32 devices in a mesh: group: 1, path: 32 (over z, y, x, core).
Axes of the slice: x: 2, y: 2, z: 4, core: 2. Of those that a mesh axis runs over, the one named last changes fastest.
Arguments:
- normals: float32 [8, 32, 8192], P(None, None, ('group', 'path')), may hold values from -6 to 6
- start_state: float32 [32, 8192], P(None, ('group', 'path')), may hold values from -0.12 to 0.12
- later_adjoint: float32 [32, 8192], P(None, ('group', 'path')), may hold values from -1.8 to 1.8
- vol: float32 [8], replicated, may hold values from 0.004 to 0.016
- factor_load: float32 [32, 960], replicated, may hold values from -2.1 to 2.1
- knots: float32 [960], replicated, may hold values from 0.01 to 0.05
- spline_jac: float32 [960, 960], replicated
- cashflows: bfloat16 [256, 960], P(('group', 'path')), may hold values from -0.1875 to 0.1875
- trade_set: int32 [256, 1], P(('group', 'path')), may hold values from 0 to 127
- trade_end: int32 [256], P(('group', 'path')), may hold values from 240 to 960
- set_cpty: int32 [128, 1], P('group'), may hold values from 0 to 63
- default_prob: float32 [8, 64], replicated, may hold values from 0.01 to 0.1
- base_value: float32 [8, 128], P(None, 'group'), may hold values from -3 to 3
Outputs:
- knot_grad: float32 [960], P('group')
- alloc: float32 [256], P(('group', 'path'))
- start_adjoint: float32 [32, 8192], P(None, ('group', 'path'))
The draws below stay inside these ranges and needn't reach their ends.
All inputs are finite; a program needn't handle non-finite values.
Results may differ from the reference program's by a relative error of at most 0.0011.
Values may be sent and summed in bfloat16 or wider, within the bound.
No kernel may reach another device: no remote copies, remote signals or barrier semaphores. Data moves between devices by JAX's collectives and lax.ppermute only.
A program may use at most 64 MiB of HBM per device.

```python
import math
import jax
import jax.numpy as jnp
from jax import lax

K = 960
FACTORS = 32
DATES = 8
CPTY = 64
PATHS = 8192
TRADES = 256
NSETS = 128


def draw_spline_jac(key, part):
    first, second = jax.random.split(jax.random.fold_in(key, 11))
    diagonal = jax.random.uniform(first, (K,), jnp.float32, 0.6, 1.0)
    spread = jax.random.normal(second, (K, K), jnp.float32) * (0.3 / math.sqrt(K))
    return jnp.diag(diagonal) + spread


def draw_trade_end(key, part):
    shuffled = jax.random.permutation(jax.random.fold_in(key, 23), TRADES).astype(jnp.int32)
    return (K // 4 + shuffled * (K - K // 4) // (TRADES - 1)).astype(jnp.int32)


def shard_levels(stream_key, shape, cuts, low, high):
    gain = 1.0
    for dim, shards_of in cuts:
        steps = jax.random.uniform(jax.random.fold_in(jax.random.fold_in(stream_key, 6), dim), (shards_of,), jnp.float32, low / len(cuts), high / len(cuts))
        gain = gain * jnp.repeat(jnp.exp(steps), shape[dim] // shards_of).reshape((-1,) + (1,) * (len(shape) - 1 - dim))
    return gain


def picks_of(stream_key, rows, count, top, lift):
    ranking = jax.random.permutation(jax.random.fold_in(stream_key, 1), count)
    favour = ranking
    for power in range(3):
        favour = favour * favour // count
    favour = favour * lift // count
    lots = jax.random.randint(jax.random.fold_in(stream_key, 2), (rows, count), 0, 4096) + favour
    sure = jax.random.permutation(jax.random.fold_in(stream_key, 3), rows)[jnp.arange(count) % rows]
    lots = jnp.where(jnp.arange(rows)[:, None] == sure[None, :], 1 << 14, lots)
    score = lots * count + jnp.arange(count)
    return lax.top_k(score.astype(jnp.int32), top)[1].astype(jnp.int32)


def normal_values(key, extent, scale, bound, cuts=(), held_as=jnp.bfloat16):
    entries = scale * jax.random.normal(key, extent, jnp.float32)
    if cuts:
        entries = entries * shard_levels(key, extent, cuts, -0.22, 0.18)
    return jnp.clip(entries, -bound, bound).astype(held_as)


def setup_inputs(seed: int = 0, part: int = 0) -> dict:
    key_of = jax.random.split(jax.random.key(seed), 14)
    part_keys = jax.random.split(jax.random.fold_in(key_of[13], part), 14)
    normals = normal_values(part_keys[0], (DATES, FACTORS, PATHS), 1.0, 6.0, ((2, 32),), jnp.float32)
    start_state = normal_values(part_keys[1], (FACTORS, PATHS), 0.02, 0.12, ((1, 32),), jnp.float32)
    later_adjoint = normal_values(part_keys[2], (FACTORS, PATHS), 0.3, 1.8, ((1, 32),), jnp.float32)
    vol = jnp.clip(jnp.exp(jax.random.uniform(key_of[3], (DATES,), jnp.float32, math.log(0.004), math.log(0.016))), 0.004, 0.016)
    factor_load = normal_values(key_of[4], (FACTORS, K), 0.35, 2.1, (), jnp.float32)
    knots = jnp.clip(jax.random.uniform(key_of[5], (K,), jnp.float32, 0.01, 0.05), 0.01, 0.05)
    spline_jac = draw_spline_jac(jax.random.fold_in(key_of[13], 71), part)
    cashflows = normal_values(part_keys[7], (TRADES, K), K ** -0.5, 0.1875, ((0, 32),))
    trade_set = picks_of(part_keys[8], TRADES, NSETS, 1, 64)
    trade_end = draw_trade_end(jax.random.fold_in(jax.random.fold_in(key_of[13], part), 71), part)
    set_cpty = picks_of(part_keys[10], NSETS, CPTY, 1, 256)
    default_prob = jnp.clip(jnp.exp(jax.random.uniform(key_of[11], (DATES, CPTY), jnp.float32, math.log(0.01), math.log(0.1))), 0.01, 0.1)
    base_value = normal_values(part_keys[12], (DATES, NSETS), 0.5, 3.0, (), jnp.float32)
    return {"normals": normals, "start_state": start_state, "later_adjoint": later_adjoint, "vol": vol, "factor_load": factor_load, "knots": knots, "spline_jac": spline_jac, "cashflows": cashflows, "trade_set": trade_set, "trade_end": trade_end, "set_cpty": set_cpty, "default_prob": default_prob, "base_value": base_value}


MEAN_REV = 0.05
STEP_YEARS = 0.25
HORIZON_YEARS = 30.0
SHARPNESS = 4.0
LOSS_RATE = 0.6


def curve_terms(knots, spline_jac, date_count, knot_count):
    zero_rate = jnp.dot(spline_jac, knots, precision=lax.Precision.HIGHEST)
    knot_index = jnp.arange(knot_count, dtype=jnp.int32)
    date_index = jnp.arange(date_count, dtype=jnp.int32)
    is_alive = (120 * (knot_index[None, :] + 1)) > (knot_count * (date_index[:, None] + 1))
    maturity = HORIZON_YEARS * (knot_index + 1).astype(jnp.float32) / knot_count
    fixing = STEP_YEARS * (date_index + 1).astype(jnp.float32)
    horizon = jnp.where(is_alive, maturity[None, :] - fixing[:, None], jnp.float32(0.0))
    loading = (1.0 - jnp.exp(-MEAN_REV * horizon)) / MEAN_REV
    discount = jnp.where(is_alive, jnp.exp(-zero_rate[None, :] * horizon), jnp.float32(0.0))
    return horizon, loading, discount


def state_path(start_state, vol, normals):
    decay_factor = math.exp(-MEAN_REV * STEP_YEARS)
    state = start_state
    collected = []
    for index in range(normals.shape[0]):
        state = decay_factor * state + vol[index] * normals[index]
        collected.append(state)
    return jnp.stack(collected)


def reference(normals, start_state, later_adjoint, vol, factor_load, knots, spline_jac, cashflows, trade_set, trade_end, set_cpty, default_prob, base_value):
    highest = lax.Precision.HIGHEST
    horizon, loading, discount = curve_terms(knots, spline_jac, DATES, K)
    knot_index = jnp.arange(K, dtype=jnp.int32)
    live_flows = jnp.where(knot_index[None, :] < trade_end[:, None], cashflows, jnp.zeros_like(cashflows))
    set_ids = trade_set[:, 0]
    net_flows = jax.ops.segment_sum(live_flows.astype(jnp.float32), set_ids, num_segments=NSETS).astype(jnp.bfloat16)
    net_wide = net_flows.astype(jnp.float32)
    weight = LOSS_RATE * default_prob[:, set_cpty[:, 0]]
    block_size = math.gcd(PATHS, 2048)
    block_count = PATHS // block_size
    states = state_path(start_state, vol, normals)
    blocked = states.reshape(DATES, FACTORS, block_count, block_size).transpose(2, 0, 1, 3)

    def block_values(block_states):
        shift = jnp.einsum('fm,ifp->imp', factor_load, block_states, precision=highest)
        bond_term = jnp.exp(-loading[:, :, None] * shift)
        feat_exact = discount[:, :, None] * bond_term
        features = feat_exact.astype(jnp.bfloat16)
        values = jnp.einsum('nm,imp->inp', net_wide, features.astype(jnp.float32), precision=highest)
        return bond_term, feat_exact, features, values

    def sum_values(running, block_states):
        return running + jnp.sum(block_values(block_states)[3], axis=2), None

    running, _ = lax.scan(sum_values, jnp.zeros((DATES, NSETS), jnp.float32), blocked)
    mean_value = running / PATHS

    def slopes(values):
        shifted = values - mean_value[:, :, None] + base_value[:, :, None]
        return weight[:, :, None] * jax.nn.sigmoid(SHARPNESS * shifted)

    def sum_slopes(running, block_states):
        return running + jnp.sum(slopes(block_values(block_states)[3]), axis=2), None

    slope_total, _ = lax.scan(sum_slopes, jnp.zeros((DATES, NSETS), jnp.float32), blocked)
    mean_slope = slope_total / PATHS

    def backward(carry, block_states):
        discount_grad, load_sums = carry
        bond_term, feat_exact, features, values = block_values(block_states)
        set_adjoint = (slopes(values) - mean_slope[:, :, None]).astype(jnp.bfloat16)
        feat_adjoint = jnp.einsum('nm,inp->imp', net_wide, set_adjoint.astype(jnp.float32), precision=highest)
        state_local = -jnp.einsum('fm,imp->ifp', factor_load, feat_adjoint * feat_exact * loading[:, :, None], precision=highest)
        discount_grad = discount_grad + jnp.sum(feat_adjoint * bond_term, axis=2)
        load_sums = load_sums + jnp.einsum('inp,imp->nm', set_adjoint.astype(jnp.float32), features.astype(jnp.float32), precision=highest)
        return (discount_grad, load_sums), state_local

    init = (jnp.zeros((DATES, K), jnp.float32), jnp.zeros((NSETS, K), jnp.float32))
    (discount_grad, load_sums), local_blocks = lax.scan(backward, init, blocked)
    state_local = local_blocks.transpose(1, 2, 0, 3).reshape(DATES, FACTORS, PATHS)
    rate_adjoint = -jnp.sum(discount_grad * discount * horizon, axis=0) / PATHS
    knot_grad = jnp.dot(spline_jac.T, rate_adjoint, precision=highest)
    load_sums = load_sums / PATHS
    alloc = jnp.sum(live_flows.astype(jnp.float32) * load_sums[set_ids], axis=1)
    decay_factor = math.exp(-MEAN_REV * STEP_YEARS)
    carried = later_adjoint + state_local[DATES - 1]
    for index in reversed(range(DATES - 1)):
        carried = state_local[index] + decay_factor * carried
    start_adjoint = decay_factor * carried
    return knot_grad, alloc, start_adjoint
```

```python
import math

import jax
import jax.numpy as jnp
from jax import lax
from jax.sharding import PartitionSpec as P

MEAN_REV = 0.05
STEP_YEARS = 0.25
HORIZON_YEARS = 30.0
SHARPNESS = 4.0
LOSS_RATE = 0.6
BASE = 128


def share(block):
    copies = jnp.broadcast_to(block[None], (lax.axis_size("path"),) + block.shape)
    return lax.all_to_all(copies, "path", 0, 0)


def curve_terms(knots, spline_jac, date_count, knot_count):
    zero_rate = jnp.dot(spline_jac, knots, precision=lax.Precision.HIGHEST)
    knot_index = jnp.arange(knot_count, dtype=jnp.int32)
    date_index = jnp.arange(date_count, dtype=jnp.int32)
    is_alive = 120 * (knot_index[None, :] + 1) > knot_count * (date_index[:, None] + 1)
    maturity = HORIZON_YEARS * (knot_index + 1).astype(jnp.float32) / knot_count
    fixing = STEP_YEARS * (date_index + 1).astype(jnp.float32)
    horizon = jnp.where(is_alive, maturity[None, :] - fixing[:, None], jnp.float32(0.0))
    loading = (1.0 - jnp.exp(-MEAN_REV * horizon)) / MEAN_REV
    discount = jnp.where(is_alive, jnp.exp(-zero_rate[None, :] * horizon), jnp.float32(0.0))
    return (horizon, loading, discount)


def state_path(start_state, vol, normals):
    decay_factor = math.exp(-MEAN_REV * STEP_YEARS)
    state = start_state
    collected = []
    for index in range(normals.shape[0]):
        state = decay_factor * state + vol[index] * normals[index]
        collected.append(state)
    return jnp.stack(collected)


def per_device(
    normals,
    start_state,
    later_adjoint,
    vol,
    factor_load,
    knots,
    spline_jac,
    cashflows,
    trade_set,
    trade_end,
    set_cpty,
    default_prob,
    base_value,
):
    highest = lax.Precision.HIGHEST
    date_count = normals.shape[0]
    knot_count = knots.shape[0]
    set_count = base_value.shape[1]
    paths_all = normals.shape[2] * lax.axis_size("path")
    horizon, loading, discount = curve_terms(knots, spline_jac, date_count, knot_count)
    knot_index = jnp.arange(knot_count, dtype=jnp.int32)
    live_flows = jnp.where(
        knot_index[None, :] < trade_end[:, None], cashflows, jnp.zeros_like(cashflows)
    )
    set_ids = trade_set[:, 0]
    labels = jnp.arange(set_count, dtype=jnp.int32)
    digits = jnp.stack([set_ids // BASE, set_ids % BASE], axis=1).astype(jnp.bfloat16)
    gathered = share(jnp.concatenate([live_flows, digits], axis=1)).reshape(-1, knot_count + 2)
    all_flows = gathered[:, :knot_count]
    all_digits = gathered[:, knot_count:].astype(jnp.int32)
    all_sets = all_digits[:, 0] * BASE + all_digits[:, 1]
    member = (labels[:, None] == all_sets[None, :]).astype(jnp.bfloat16)
    net_flows = jnp.dot(member, all_flows, preferred_element_type=jnp.float32).astype(jnp.bfloat16)
    counter = (
        jnp.arange(default_prob.shape[1], dtype=jnp.int32)[:, None] == set_cpty[:, 0][None, :]
    ).astype(jnp.float32)
    weight = LOSS_RATE * jnp.dot(default_prob, counter, precision=highest)
    states = state_path(start_state, vol, normals)
    shift = jnp.einsum("fm,ifp->imp", factor_load, states, precision=highest)
    bond_term = jnp.exp(-loading[:, :, None] * shift)
    feat_exact = discount[:, :, None] * bond_term
    features = feat_exact.astype(jnp.bfloat16)
    values = jnp.einsum("nm,imp->inp", net_flows, features, preferred_element_type=jnp.float32)
    mean_value = jnp.sum(share(jnp.sum(values, axis=2)), axis=0) / paths_all
    shifted = values - mean_value[:, :, None] + base_value[:, :, None]
    slope = weight[:, :, None] * jax.nn.sigmoid(SHARPNESS * shifted)
    mean_slope = jnp.sum(share(jnp.sum(slope, axis=2)), axis=0) / paths_all
    set_adjoint = (slope - mean_slope[:, :, None]).astype(jnp.bfloat16)
    feat_adjoint = jnp.einsum(
        "nm,inp->imp", net_flows, set_adjoint, preferred_element_type=jnp.float32
    )
    state_local = -jnp.einsum(
        "fm,imp->ifp",
        factor_load,
        feat_adjoint * feat_exact * loading[:, :, None],
        precision=highest,
    )
    discount_grad = jnp.sum(feat_adjoint * bond_term, axis=2)
    rate_adjoint = -jnp.sum(discount_grad * discount * horizon, axis=0) / paths_all
    load_sums = (
        jnp.einsum("inp,imp->nm", set_adjoint, features, preferred_element_type=jnp.float32)
        / paths_all
    )
    spread = jnp.dot(member.T, load_sums, precision=highest)
    trade_part = jnp.sum(all_flows.astype(jnp.float32) * spread, axis=1)
    shard_count = lax.axis_size("path")
    packed = jnp.concatenate(
        [
            jnp.broadcast_to(rate_adjoint[None], (shard_count, knot_count)),
            trade_part.reshape(shard_count, -1),
        ],
        axis=1,
    )
    summed = jnp.sum(lax.all_to_all(packed[:, None], "path", 0, 0), axis=0)[0]
    rate_total, alloc = summed[:knot_count], summed[knot_count:]
    knot_grad = jnp.dot(spline_jac.T, rate_total, precision=highest)
    decay_factor = math.exp(-MEAN_REV * STEP_YEARS)
    carried = later_adjoint + state_local[date_count - 1]
    for index in reversed(range(date_count - 1)):
        carried = state_local[index] + decay_factor * carried
    start_adjoint = decay_factor * carried
    return (knot_grad, alloc, start_adjoint)


def solution(mesh):
    in_specs = (
        P(None, None, ("group", "path")),
        P(None, ("group", "path")),
        P(None, ("group", "path")),
        P(),
        P(),
        P(),
        P(),
        P(("group", "path"), None),
        P(("group", "path"), None),
        P(("group", "path")),
        P("group", None),
        P(),
        P(None, "group"),
    )
    out_specs = (P("group"), P(("group", "path")), P(None, ("group", "path")))
    return jax.shard_map(
        per_device, mesh=mesh, in_specs=in_specs, out_specs=out_specs, check_vma=False
    )
```

```python
import functools
import math

import jax
import jax.numpy as jnp
from jax import lax
from jax.experimental import pallas as pl
from jax.experimental.pallas import tpu as pltpu
from jax.sharding import PartitionSpec as P

MEAN_REV = 0.05
STEP_YEARS = 0.25
HORIZON_YEARS = 30.0
SHARPNESS = 4.0
LOSS_RATE = 0.6
BASE = 128
LANES = 128
DECAY = math.exp(-MEAN_REV * STEP_YEARS)
HIGHEST = lax.Precision.HIGHEST
F32 = jnp.float32
BF16 = jnp.bfloat16


def round_up(size, step):
    return -(-size // step) * step


def exchange(copies):
    return lax.all_to_all(copies, "path", 0, 0)


def split(value, terms):
    parts = []
    for _ in range(terms):
        part = value.astype(BF16)
        parts.append(part)
        value = value - part.astype(F32)
    return parts


def contract(lhs, rhs, lhs_dim, rhs_dim, precision=None):
    return lax.dot_general(
        lhs,
        rhs,
        (((lhs_dim,), (rhs_dim,)), ((), ())),
        precision=precision,
        preferred_element_type=F32,
    )


def date_rows(date, knot_count):
    point = lax.broadcasted_iota(jnp.int32, (1, knot_count), 1) + 1
    alive = 120 * point > knot_count * (date + 1)
    maturity = HORIZON_YEARS * point.astype(F32) / knot_count
    fixing = STEP_YEARS * (date + 1).astype(F32)
    horizon = jnp.where(alive, maturity - fixing, 0.0)
    loading = (1.0 - jnp.exp(-MEAN_REV * horizon)) / MEAN_REV
    return alive, horizon, loading


def member_rows(flows, knot_count, set_count):
    digits = flows[:, knot_count : knot_count + 2].astype(F32)
    sets = (digits[:, 0:1] * BASE + digits[:, 1:2]).astype(jnp.int32)
    labels = lax.broadcasted_iota(jnp.int32, (flows.shape[0], set_count), 1)
    return sets == labels


def prep_kernel(end_ref, set_ref, cash_ref, out_ref):
    shards, trades, width = out_ref.shape
    knot_count = cash_ref.shape[1]
    row = lax.broadcasted_iota(jnp.int32, (trades, width), 0)
    point = lax.broadcasted_iota(jnp.int32, (trades, width), 1)
    ends = jnp.zeros((trades, width), jnp.int32)
    sets = jnp.zeros((trades, width), jnp.int32)
    for trade in range(trades):
        ends = jnp.where(row == trade, end_ref[trade], ends)
        sets = jnp.where(row == trade, set_ref[trade, 0], sets)
    cash = jnp.concatenate(
        [cash_ref[...].astype(F32), jnp.zeros((trades, width - knot_count), F32)], axis=1
    )
    high = lax.shift_right_logical(sets, BASE.bit_length() - 1)
    low = sets & (BASE - 1)
    flows = jnp.where(point < jnp.minimum(ends, knot_count), cash, 0.0)
    flows = jnp.where(point == knot_count, high.astype(F32), flows)
    flows = jnp.where(point == knot_count + 1, low.astype(F32), flows).astype(BF16)
    for shard in range(shards):
        out_ref[shard] = flows


def curve_kernel(knots_ref, jac_ref, cpty_ref, prob_ref, rate_ref, weight_ref):
    knot_count = jac_ref.shape[0]
    column = jnp.sum(jac_ref[...] * knots_ref[...], axis=1, keepdims=True)
    rate_ref[...] = jnp.broadcast_to(column, (knot_count, LANES)).T[0:1]
    sets, counterparties = cpty_ref.shape[0], prob_ref.shape[1]
    labels = lax.broadcasted_iota(jnp.int32, (sets, counterparties), 1)
    chosen = (cpty_ref[...] == labels).astype(F32)
    weight_ref[...] = LOSS_RATE * contract(prob_ref[...], chosen, 1, 1, HIGHEST)


def feature_kernel(vol_ref, normals_ref, start_ref, load_ref, rate_ref, exact_ref, feat_ref, state, stacked):
    date = pl.program_id(0)
    knot_count = load_ref.shape[1]

    @pl.when(date == 0)
    def _():
        state[...] = start_ref[...]
        high, middle, low = split(load_ref[...], 3)
        stacked[...] = jnp.concatenate([high, middle, high, middle, low, high], axis=0)

    now = DECAY * state[...] + vol_ref[date] * normals_ref[0]
    state[...] = now
    high, middle, low = split(now, 3)
    terms = jnp.concatenate([high, high, middle, middle, high, low], axis=0)
    alive, horizon, loading = date_rows(date, knot_count)
    discount = jnp.where(alive, jnp.exp(-rate_ref[...] * horizon), 0.0)
    shift = contract(terms, stacked[...], 0, 0)
    exact = discount * jnp.exp(-loading * shift)
    exact_ref[0] = exact
    feat_ref[0] = exact.astype(BF16)


def value_kernel(flows_ref, feat_ref, values_ref, net_ref, out_ref, sums):
    date = pl.program_id(0)
    knot_count = feat_ref.shape[2]

    @pl.when(date == 0)
    def _():
        flows = flows_ref[...]
        member = member_rows(flows, knot_count, net_ref.shape[0]).astype(BF16)
        net_ref[...] = contract(member, flows[:, :knot_count], 0, 0).astype(BF16)

    values = contract(feat_ref[0], net_ref[...], 1, 1)
    values_ref[0] = values
    sums[pl.ds(date, 1), :] = jnp.sum(values, axis=0, keepdims=True)

    @pl.when(date == pl.num_programs(0) - 1)
    def _():
        out_ref[...] = jnp.broadcast_to(sums[...][None], out_ref.shape)


def slope_kernel(paths, arrived_ref, values_ref, weight_ref, base_ref, slope_ref, out_ref, sums):
    mean = jnp.sum(arrived_ref[...], axis=0) / paths
    for date in range(values_ref.shape[0]):
        row = slice(date, date + 1)
        shifted = values_ref[date] - mean[row] + base_ref[row, :]
        slope = weight_ref[row, :] * jax.nn.sigmoid(SHARPNESS * shifted)
        slope_ref[date] = slope
        sums[row, :] = jnp.sum(slope, axis=0, keepdims=True)
    out_ref[...] = jnp.broadcast_to(sums[...][None], out_ref.shape)


def adjoint_kernel(paths, arrived_ref, slope_ref, exact_ref, net_ref, flows_ref, blend_ref, out_ref, mean, rate, loads):
    date = pl.program_id(0)
    knot_count = exact_ref.shape[2]

    @pl.when(date == 0)
    def _():
        mean[...] = jnp.sum(arrived_ref[...], axis=0) / paths
        blend_ref[...] = jnp.zeros_like(blend_ref)
        rate[...] = jnp.zeros_like(rate)
        loads[...] = jnp.zeros_like(loads)

    _, horizon, loading = date_rows(date, knot_count)
    factor = loading * jnp.exp(-MEAN_REV * STEP_YEARS * (date + 1).astype(F32))
    exact = exact_ref[0]
    adjoint = (slope_ref[0] - mean[pl.ds(date, 1), :]).astype(BF16)
    product = contract(adjoint, net_ref[...], 1, 0) * exact
    blend_ref[...] += factor * product
    rate[...] += horizon * jnp.sum(product.reshape(-1, 8, knot_count), axis=0)
    loads[...] += contract(adjoint, exact.astype(BF16), 0, 0)

    @pl.when(date == pl.num_programs(0) - 1)
    def _():
        flows = flows_ref[...]
        member = member_rows(flows, knot_count, net_ref.shape[0])
        shares = jnp.zeros(member.shape, F32)
        for part in split(loads[...], 3):
            shares = shares + contract(flows[:, :knot_count], part, 1, 1)
        trades = jnp.sum(jnp.where(member, shares, 0.0).T, axis=0, keepdims=True) / paths
        total = -jnp.sum(rate[...], axis=0, keepdims=True) / paths
        shards, _, width = out_ref.shape
        gap = jnp.zeros((1, width - knot_count - trades.shape[1]), F32)
        row = jnp.concatenate([total, gap, trades], axis=1)
        out_ref[...] = jnp.broadcast_to(row[None], out_ref.shape)


def start_kernel(dates, blend_ref, load_ref, later_ref, out_ref):
    carried = contract(load_ref[...], blend_ref[...], 1, 1, HIGHEST)
    out_ref[...] = math.exp(-MEAN_REV * STEP_YEARS * dates) * later_ref[...] - carried


def final_kernel(index_ref, arrived_ref, jac_ref, knot_ref, alloc_ref):
    knot_count = jac_ref.shape[0]
    trades = alloc_ref.shape[1]
    row = jnp.sum(arrived_ref[...], axis=0)
    parts = row[:, round_up(knot_count, LANES) :]
    total = parts.shape[1]
    parts = jnp.broadcast_to(parts, (8, total))
    offset = index_ref[0] * trades
    alloc_ref[...] = pltpu.roll(parts, lax.rem(total - offset, total), 1)[0:1, :trades]
    column = jnp.broadcast_to(row[:, :knot_count], (LANES, knot_count)).T
    for first in range(0, knot_count, LANES):
        size = min(LANES, knot_count - first)
        cut = slice(first, first + size)
        knot_ref[:, cut] = jnp.sum(jac_ref[:, cut] * column[:, :size], axis=0, keepdims=True)


VMEM = pl.BlockSpec(memory_space=pltpu.VMEM)
SMEM = pl.BlockSpec(memory_space=pltpu.SMEM)


def whole(shape):
    return pl.BlockSpec(shape, lambda date: (0,) * len(shape))


def dated(shape):
    return pl.BlockSpec((1,) + shape, lambda date: (date,) + (0,) * len(shape))


def shaped(shape, dtype=F32):
    return jax.ShapeDtypeStruct(shape, dtype)


def cost(flops, moved):
    return pl.CostEstimate(flops=flops, bytes_accessed=moved, transcendentals=0)


def per_device(
    normals,
    start_state,
    later_adjoint,
    vol,
    factor_load,
    knots,
    spline_jac,
    cashflows,
    trade_set,
    trade_end,
    set_cpty,
    default_prob,
    base_value,
):
    dates, factors, paths = normals.shape
    knot_count = knots.shape[0]
    sets = base_value.shape[1]
    shards = lax.axis_size("path")
    trades = cashflows.shape[0]
    all_trades = trades * shards
    all_paths = paths * shards
    width = round_up(knot_count + 2, LANES)
    work = 2 * dates * paths * knot_count

    copies = pl.pallas_call(
        prep_kernel,
        out_shape=shaped((shards, trades, width), BF16),
        in_specs=[SMEM, SMEM, VMEM],
        out_specs=VMEM,
        name="prep",
    )(trade_end, trade_set, cashflows)
    flows = exchange(copies).reshape(all_trades, width)

    zero_rate, weight = pl.pallas_call(
        curve_kernel,
        out_shape=(shaped((1, knot_count)), shaped((dates, sets))),
        in_specs=[VMEM] * 4,
        out_specs=(VMEM, VMEM),
        cost_estimate=cost(2 * knot_count**2, 4 * knot_count**2),
        name="curve",
    )(knots.reshape(1, knot_count), spline_jac, set_cpty, default_prob)

    exact, features = pl.pallas_call(
        feature_kernel,
        out_shape=(
            shaped((dates, paths, knot_count)),
            shaped((dates, paths, knot_count), BF16),
        ),
        grid=(dates,),
        in_specs=[
            SMEM,
            dated((factors, paths)),
            whole((factors, paths)),
            whole((factors, knot_count)),
            whole((1, knot_count)),
        ],
        out_specs=(dated((paths, knot_count)), dated((paths, knot_count))),
        scratch_shapes=[
            pltpu.VMEM((factors, paths), F32),
            pltpu.VMEM((6 * factors, knot_count), BF16),
        ],
        cost_estimate=cost(6 * factors * work, 4 * work),
        name="features",
    )(vol, normals, start_state, factor_load, zero_rate)

    values, net_flows, copies = pl.pallas_call(
        value_kernel,
        out_shape=(
            shaped((dates, paths, sets)),
            shaped((sets, knot_count), BF16),
            shaped((shards, dates, sets)),
        ),
        grid=(dates,),
        in_specs=[whole((all_trades, width)), dated((paths, knot_count))],
        out_specs=(
            dated((paths, sets)),
            whole((sets, knot_count)),
            whole((shards, dates, sets)),
        ),
        scratch_shapes=[pltpu.VMEM((dates, sets), F32)],
        cost_estimate=cost(sets * work, 2 * work),
        name="values",
    )(flows, features)

    slope, copies = pl.pallas_call(
        functools.partial(slope_kernel, all_paths),
        out_shape=(shaped((dates, paths, sets)), shaped((shards, dates, sets))),
        in_specs=[VMEM] * 4,
        out_specs=(VMEM, VMEM),
        scratch_shapes=[pltpu.VMEM((dates, sets), F32)],
        cost_estimate=cost(16 * dates * paths * sets, 8 * dates * paths * sets),
        name="slopes",
    )(exchange(copies), values, weight, base_value)

    row_width = round_up(knot_count, LANES) + all_trades
    blend, copies = pl.pallas_call(
        functools.partial(adjoint_kernel, all_paths),
        out_shape=(shaped((paths, knot_count)), shaped((shards, 1, row_width))),
        grid=(dates,),
        in_specs=[
            whole((shards, dates, sets)),
            dated((paths, sets)),
            dated((paths, knot_count)),
            whole((sets, knot_count)),
            whole((all_trades, width)),
        ],
        out_specs=(whole((paths, knot_count)), whole((shards, 1, row_width))),
        scratch_shapes=[
            pltpu.VMEM((dates, sets), F32),
            pltpu.VMEM((8, knot_count), F32),
            pltpu.VMEM((sets, knot_count), F32),
        ],
        cost_estimate=cost(2 * sets * work, 4 * work),
        name="adjoint",
    )(exchange(copies), slope, exact, net_flows, flows)

    arrived = exchange(copies)
    start_adjoint = pl.pallas_call(
        functools.partial(start_kernel, dates),
        out_shape=shaped((factors, paths)),
        in_specs=[VMEM] * 3,
        out_specs=VMEM,
        cost_estimate=cost(2 * factors * paths * knot_count, 4 * paths * knot_count),
        name="start",
    )(blend, factor_load, later_adjoint)

    index = lax.axis_index("path").astype(jnp.int32).reshape(1)
    knot_grad, alloc = pl.pallas_call(
        final_kernel,
        out_shape=(shaped((1, knot_count)), shaped((1, trades))),
        in_specs=[SMEM, VMEM, VMEM],
        out_specs=(VMEM, VMEM),
        cost_estimate=cost(2 * knot_count**2, 4 * knot_count**2),
        name="final",
    )(index, arrived, spline_jac)
    return knot_grad.reshape(knot_count), alloc.reshape(trades), start_adjoint


def solution(mesh):
    in_specs = (
        P(None, None, ("group", "path")),
        P(None, ("group", "path")),
        P(None, ("group", "path")),
        P(),
        P(),
        P(),
        P(),
        P(("group", "path"), None),
        P(("group", "path"), None),
        P(("group", "path")),
        P("group", None),
        P(),
        P(None, "group"),
    )
    out_specs = (P("group"), P(("group", "path")), P(None, ("group", "path")))
    return jax.shard_map(
        per_device, mesh=mesh, in_specs=in_specs, out_specs=out_specs, check_vma=False
    )
```

```python
import functools
import math

import jax
import jax.numpy as jnp
from jax import lax
from jax.experimental import pallas as pl
from jax.experimental.pallas import tpu as pltpu
from jax.sharding import PartitionSpec as P

MEAN_REV = 0.05
STEP_YEARS = 0.25
HORIZON_YEARS = 30.0
SHARPNESS = 4.0
LOSS_RATE = 0.6
BASE = 128
LANES = 128
DECAY = math.exp(-MEAN_REV * STEP_YEARS)
HIGHEST = lax.Precision.HIGHEST
F32 = jnp.float32
BF16 = jnp.bfloat16


def round_up(size, step):
    return -(-size // step) * step


def exchange(copies):
    return lax.all_to_all(copies, "path", 0, 0)


def split(value, terms):
    parts = []
    for _ in range(terms):
        part = value.astype(BF16)
        parts.append(part)
        value = value - part.astype(F32)
    return parts


def contract(lhs, rhs, lhs_dim, rhs_dim, precision=None):
    return lax.dot_general(
        lhs,
        rhs,
        (((lhs_dim,), (rhs_dim,)), ((), ())),
        precision=precision,
        preferred_element_type=F32,
    )


def date_rows(date, knot_count):
    point = lax.broadcasted_iota(jnp.int32, (1, knot_count), 1) + 1
    alive = 120 * point > knot_count * (date + 1)
    maturity = HORIZON_YEARS * point.astype(F32) / knot_count
    fixing = STEP_YEARS * (date + 1).astype(F32)
    horizon = jnp.where(alive, maturity - fixing, 0.0)
    loading = (1.0 - jnp.exp(-MEAN_REV * horizon)) / MEAN_REV
    return alive, horizon, loading


def member_rows(flows, knot_count, set_count):
    digits = flows[:, knot_count : knot_count + 2].astype(F32)
    sets = (digits[:, 0:1] * BASE + digits[:, 1:2]).astype(jnp.int32)
    labels = lax.broadcasted_iota(jnp.int32, (flows.shape[0], set_count), 1)
    return sets == labels


def prep_kernel(end_ref, set_ref, cash_ref, out_ref):
    shards, trades, width = out_ref.shape
    knot_count = cash_ref.shape[1]
    row = lax.broadcasted_iota(jnp.int32, (trades, width), 0)
    point = lax.broadcasted_iota(jnp.int32, (trades, width), 1)
    ends = jnp.zeros((trades, width), jnp.int32)
    sets = jnp.zeros((trades, width), jnp.int32)
    for trade in range(trades):
        ends = jnp.where(row == trade, end_ref[trade], ends)
        sets = jnp.where(row == trade, set_ref[trade], sets)
    cash = jnp.concatenate(
        [cash_ref[...].astype(F32), jnp.zeros((trades, width - knot_count), F32)], axis=1
    )
    high = lax.shift_right_logical(sets, BASE.bit_length() - 1)
    low = sets & (BASE - 1)
    flows = jnp.where(point < jnp.minimum(ends, knot_count), cash, 0.0)
    flows = jnp.where(point == knot_count, high.astype(F32), flows)
    flows = jnp.where(point == knot_count + 1, low.astype(F32), flows).astype(BF16)
    for shard in range(shards):
        out_ref[shard] = flows


def curve_kernel(knots_ref, jac_ref, cpty_ref, prob_ref, rate_ref, weight_ref):
    knot_count = jac_ref.shape[0]
    column = jnp.sum(jac_ref[...] * knots_ref[...], axis=1, keepdims=True)
    rate_ref[...] = jnp.broadcast_to(column, (knot_count, LANES)).T[0:1]
    labels = lax.broadcasted_iota(jnp.int32, (prob_ref.shape[1], cpty_ref.shape[1]), 0)
    chosen = (cpty_ref[...] == labels).astype(F32)
    weight_ref[...] = LOSS_RATE * contract(prob_ref[...], chosen, 1, 0, HIGHEST)


def feature_kernel(
    vol_ref, normals_ref, start_ref, load_ref, rate_ref,
    exact_ref, feat_ref, exact_sum_ref, feat_sum_ref, state, stacked,
):
    date = pl.program_id(0)
    knot_count = load_ref.shape[1]

    @pl.when(date == 0)
    def _():
        state[...] = start_ref[...]
        high, middle, low = split(load_ref[...], 3)
        stacked[...] = jnp.concatenate([high, middle, high, middle, low, high], axis=0)

    now = DECAY * state[...] + vol_ref[date] * normals_ref[0]
    state[...] = now
    high, middle, low = split(now, 3)
    terms = jnp.concatenate([high, high, middle, middle, high, low], axis=0)
    alive, horizon, loading = date_rows(date, knot_count)
    discount = jnp.where(alive, jnp.exp(-rate_ref[...] * horizon), 0.0)
    shift = contract(terms, stacked[...], 0, 0)
    exact = discount * jnp.exp(-loading * shift)
    exact_ref[0] = exact
    rounded = exact.astype(BF16)
    feat_ref[0] = rounded
    row = pl.ds(date, 1)
    exact_sum_ref[row, :] = jnp.sum(exact, axis=0, keepdims=True)
    feat_sum_ref[row, :] = jnp.sum(rounded.astype(F32), axis=0, keepdims=True)


def net_kernel(flows_ref, feat_sum_ref, net_ref, out_ref):
    knot_count, sets = net_ref.shape
    flows = flows_ref[...]
    member = member_rows(flows, knot_count, sets).astype(BF16)
    net = contract(flows[:, :knot_count], member, 0, 0).astype(BF16)
    net_ref[...] = net
    sums = jnp.zeros(out_ref.shape[1:], F32)
    for part in split(feat_sum_ref[...], 3):
        sums = sums + contract(part, net, 1, 0)
    out_ref[...] = jnp.broadcast_to(sums[None], out_ref.shape)


def value_kernel(flows_ref, net_ref, feat_ref, values_ref, rows_ref):
    values_ref[0] = contract(feat_ref[0], net_ref[...], 1, 0)

    @pl.when(pl.program_id(0) == 0)
    def _():
        sets, knot_count = rows_ref.shape
        flows = flows_ref[...]
        member = member_rows(flows, knot_count, sets).astype(BF16)
        rows_ref[...] = contract(member, flows[:, :knot_count], 0, 0).astype(BF16)


def slope_of(values, mean, base, weight):
    return weight * jax.nn.sigmoid(SHARPNESS * (values - mean + base))


def slope_kernel(paths, arrived_ref, values_ref, weight_ref, base_ref, mean_ref, sums_ref, out_ref):
    mean_ref[...] = jnp.sum(arrived_ref[...], axis=0) / paths
    for date in range(values_ref.shape[0]):
        row = slice(date, date + 1)
        slope = slope_of(values_ref[date], mean_ref[row, :], base_ref[row, :], weight_ref[row, :])
        sums_ref[row, :] = jnp.sum(slope, axis=0, keepdims=True)
    out_ref[...] = jnp.broadcast_to(sums_ref[...][None], out_ref.shape)


def adjoint_kernel(
    mean_ref, sums_ref, weight_ref, base_ref, feat_sum_ref, values_ref, exact_ref, net_ref, flows_ref,
    blend_ref, rate_ref, trades_ref, cross_ref, rate, loads,
):
    date = pl.program_id(0)
    paths, knot_count = blend_ref.shape

    @pl.when(date == 0)
    def _():
        blend_ref[...] = jnp.zeros_like(blend_ref)
        rate[...] = jnp.zeros_like(rate)
        loads[...] = jnp.zeros_like(loads)

    _, horizon, loading = date_rows(date, knot_count)
    factor = loading * jnp.exp(-MEAN_REV * STEP_YEARS * (date + 1).astype(F32))
    exact = exact_ref[0]
    row = pl.ds(date, 1)
    slope = slope_of(values_ref[0], mean_ref[row, :], base_ref[row, :], weight_ref[row, :])
    adjoint = (slope - sums_ref[row, :] / paths).astype(BF16)
    product = contract(adjoint, net_ref[...], 1, 0) * exact
    blend_ref[...] += factor * product
    rate[...] += horizon * jnp.sum(product.reshape(-1, 8, knot_count), axis=0)
    loads[...] += contract(adjoint, exact.astype(BF16), 0, 0)

    @pl.when(date == pl.num_programs(0) - 1)
    def _():
        flows = flows_ref[...]
        member = member_rows(flows, knot_count, net_ref.shape[0])
        flows = flows[:, :knot_count]
        shares = jnp.zeros(member.shape, F32)
        for part in split(loads[...], 3):
            shares = shares + contract(flows, part, 1, 1)
        trades_ref[...] = jnp.sum(jnp.where(member, shares, 0.0).T, axis=0, keepdims=True)
        rate_ref[...] = jnp.sum(rate[...], axis=0, keepdims=True)
        cross = jnp.zeros(cross_ref.shape, F32)
        for part in split(feat_sum_ref[...], 3):
            cross = cross + contract(part, flows, 1, 1)
        cross_ref[...] = cross


def finish_kernel(
    paths, local, arrived_ref, sums_ref, exact_sum_ref, net_ref, flows_ref, rate_ref, trades_ref, cross_ref,
    shift_ref, out_ref,
):
    sets, knot_count = net_ref.shape
    gap = sums_ref[...] / local - jnp.sum(arrived_ref[...], axis=0) / paths
    flows = flows_ref[...]
    member = member_rows(flows, knot_count, sets).astype(BF16)
    spread = jnp.zeros(cross_ref.shape, F32)
    adjoint = jnp.zeros(shift_ref.shape, F32)
    for part in split(gap, 3):
        spread = spread + contract(part, member, 1, 1)
        adjoint = adjoint + contract(part, net_ref[...], 1, 0)
    total = rate_ref[...]
    for date in range(shift_ref.shape[0]):
        row = slice(date, date + 1)
        _, horizon, loading = date_rows(jnp.int32(date), knot_count)
        shift_ref[row, :] = loading * math.exp(-MEAN_REV * STEP_YEARS * (date + 1)) * adjoint[row]
        total = total + horizon * adjoint[row] * exact_sum_ref[row, :]
    trades = trades_ref[...] + jnp.sum(spread * cross_ref[...], axis=0, keepdims=True)
    shards, _, width = out_ref.shape
    pad = jnp.zeros((1, width - knot_count - trades.shape[1]), F32)
    row = jnp.concatenate([-total / paths, pad, trades / paths], axis=1)
    out_ref[...] = jnp.broadcast_to(row[None], out_ref.shape)


def start_kernel(blend_ref, shift_ref, exact_ref, load_ref, later_ref, out_ref, blend):
    date = pl.program_id(0)
    dates = shift_ref.shape[0]

    @pl.when(date == 0)
    def _():
        blend[...] = blend_ref[...]

    blend[...] += shift_ref[pl.ds(date, 1), :] * exact_ref[0]

    @pl.when(date == dates - 1)
    def _():
        carried = contract(load_ref[...], blend[...], 1, 1, HIGHEST)
        out_ref[...] = math.exp(-MEAN_REV * STEP_YEARS * dates) * later_ref[...] - carried


def final_kernel(index_ref, arrived_ref, jac_ref, knot_ref, alloc_ref):
    knot_count = jac_ref.shape[0]
    trades = alloc_ref.shape[1]
    row = jnp.sum(arrived_ref[...], axis=0)
    parts = row[:, round_up(knot_count, LANES) :]
    total = parts.shape[1]
    parts = jnp.broadcast_to(parts, (8, total))
    offset = index_ref[0] * trades
    alloc_ref[...] = pltpu.roll(parts, lax.rem(total - offset, total), 1)[0:1, :trades]
    column = jnp.broadcast_to(row[:, :knot_count], (LANES, knot_count)).T
    for first in range(0, knot_count, LANES):
        size = min(LANES, knot_count - first)
        cut = slice(first, first + size)
        knot_ref[:, cut] = jnp.sum(jac_ref[:, cut] * column[:, :size], axis=0, keepdims=True)


VMEM = pl.BlockSpec(memory_space=pltpu.VMEM)
SMEM = pl.BlockSpec(memory_space=pltpu.SMEM)


def shaped(shape, dtype=F32):
    return jax.ShapeDtypeStruct(shape, dtype)


def held(array):
    size = array.dtype.itemsize
    rows = array.shape[-2] if len(array.shape) > 1 else 1
    lead = math.prod(array.shape[:-2])
    return lead * round_up(rows, 8) * round_up(array.shape[-1], LANES) * size


def run(name, kernel, out_shape, operands, scalars=0, dates=0, dated=(), scratch=(), flops=0, spare=8 << 20):
    arrays = list(operands) + list(out_shape)
    room = sum(held(array) for array in scratch) + spare
    specs = []
    for place, array in enumerate(arrays):
        if place < scalars:
            specs.append(SMEM)
        elif not dates:
            specs.append(VMEM)
            room += held(array)
        elif place in dated:
            tail = array.shape[1:]
            specs.append(pl.BlockSpec((1,) + tail, lambda date, n=len(tail): (date,) + (0,) * n))
            room += 2 * held(array) // dates
        else:
            specs.append(pl.BlockSpec(array.shape, lambda date, n=len(array.shape): (0,) * n))
            room += 2 * held(array)
    moved = sum(held(array) for array in arrays)
    return pl.pallas_call(
        kernel,
        out_shape=tuple(out_shape),
        grid=(dates,) if dates else (),
        in_specs=specs[: len(operands)],
        out_specs=tuple(specs[len(operands) :]),
        scratch_shapes=[pltpu.VMEM(array.shape, array.dtype) for array in scratch],
        compiler_params=pltpu.CompilerParams(vmem_limit_bytes=min(room, 60 << 20)),
        cost_estimate=pl.CostEstimate(flops=flops, bytes_accessed=moved, transcendentals=0),
        name=name,
    )(*operands)


def per_device(
    normals,
    start_state,
    later_adjoint,
    vol,
    factor_load,
    knots,
    spline_jac,
    cashflows,
    trade_set,
    trade_end,
    set_cpty,
    default_prob,
    base_value,
):
    dates, factors, paths = normals.shape
    knot_count = knots.shape[0]
    sets = base_value.shape[1]
    shards = lax.axis_size("path")
    trades = cashflows.shape[0]
    all_trades = trades * shards
    all_paths = paths * shards
    width = round_up(knot_count + 2, LANES)
    work = 2 * dates * paths * knot_count
    grid_rows = shaped((dates, knot_count))
    set_rows = shaped((dates, sets))
    set_copies = shaped((shards, dates, sets))

    (copies,) = run(
        "prep",
        prep_kernel,
        [shaped((shards, trades, width), BF16)],
        [trade_end, trade_set.reshape(trades), cashflows],
        scalars=2,
    )
    arrived = exchange(copies)

    zero_rate, weight = run(
        "curve",
        curve_kernel,
        [shaped((1, knot_count)), set_rows],
        [knots.reshape(1, knot_count), spline_jac, set_cpty.reshape(1, sets), default_prob],
        flops=2 * knot_count**2,
    )
    exact, features, exact_sums, feat_sums = run(
        "features",
        feature_kernel,
        [
            shaped((dates, paths, knot_count)),
            shaped((dates, paths, knot_count), BF16),
            grid_rows,
            grid_rows,
        ],
        [vol, normals, start_state, factor_load, zero_rate],
        scalars=1,
        dates=dates,
        dated=(1, 5, 6),
        scratch=[shaped((factors, paths)), shaped((6 * factors, knot_count), BF16)],
        flops=6 * factors * work,
    )

    flows = arrived.reshape(all_trades, width)
    net_columns, copies = run(
        "net",
        net_kernel,
        [shaped((knot_count, sets), BF16), set_copies],
        [flows, feat_sums],
        flops=2 * sets * all_trades * knot_count,
    )
    arrived = exchange(copies)
    values, net_rows = run(
        "values",
        value_kernel,
        [shaped((dates, paths, sets)), shaped((sets, knot_count), BF16)],
        [flows, net_columns, features],
        dates=dates,
        dated=(2, 3),
        flops=sets * work,
    )
    mean, slope_sums, copies = run(
        "slopes",
        functools.partial(slope_kernel, all_paths),
        [set_rows, set_rows, set_copies],
        [arrived, values, weight, base_value],
        flops=16 * dates * paths * sets,
    )
    arrived = exchange(copies)
    blend, rate, trade_parts, cross = run(
        "adjoint",
        adjoint_kernel,
        [
            shaped((paths, knot_count)),
            shaped((1, knot_count)),
            shaped((1, all_trades)),
            shaped((dates, all_trades)),
        ],
        [mean, slope_sums, weight, base_value, feat_sums, values, exact, net_rows, flows],
        dates=dates,
        dated=(5, 6),
        scratch=[shaped((8, knot_count)), shaped((sets, knot_count))],
        flops=2 * sets * work,
    )
    row_width = round_up(knot_count, LANES) + all_trades
    shift, copies = run(
        "finish",
        functools.partial(finish_kernel, all_paths, paths),
        [grid_rows, shaped((shards, 1, row_width))],
        [arrived, slope_sums, exact_sums, net_rows, flows, rate, trade_parts, cross],
        flops=6 * sets * dates * knot_count,
    )
    arrived = exchange(copies)
    (start_adjoint,) = run(
        "start",
        start_kernel,
        [shaped((factors, paths))],
        [blend, shift, exact, factor_load, later_adjoint],
        dates=dates,
        dated=(2,),
        scratch=[shaped((paths, knot_count))],
        flops=2 * factors * paths * knot_count,
    )
    index = lax.axis_index("path").astype(jnp.int32).reshape(1)
    knot_grad, alloc = run(
        "final",
        final_kernel,
        [shaped((1, knot_count)), shaped((1, trades))],
        [index, arrived, spline_jac],
        scalars=1,
        flops=2 * knot_count**2,
    )
    return knot_grad.reshape(knot_count), alloc.reshape(trades), start_adjoint


def solution(mesh):
    in_specs = (
        P(None, None, ("group", "path")),
        P(None, ("group", "path")),
        P(None, ("group", "path")),
        P(),
        P(),
        P(),
        P(),
        P(("group", "path"), None),
        P(("group", "path"), None),
        P(("group", "path")),
        P("group", None),
        P(),
        P(None, "group"),
    )
    out_specs = (P("group"), P(("group", "path")), P(None, ("group", "path")))
    return jax.shard_map(
        per_device, mesh=mesh, in_specs=in_specs, out_specs=out_specs, check_vma=False
    )
```

```python
import functools
import math

import jax
import jax.numpy as jnp
from jax import lax
from jax.experimental import pallas as pl
from jax.experimental.pallas import tpu as pltpu
from jax.sharding import PartitionSpec as P

MEAN_REV = 0.05
STEP_YEARS = 0.25
HORIZON_YEARS = 30.0
SHARPNESS = 4.0
LOSS_RATE = 0.6
BASE = 128
LANES = 128
LARGE = 58 << 20
MIDDLE = 50 << 20
DECAY = math.exp(-MEAN_REV * STEP_YEARS)
HIGHEST = lax.Precision.HIGHEST
F32 = jnp.float32
BF16 = jnp.bfloat16


def round_up(size, step):
    return -(-size // step) * step


def exchange(copies):
    return lax.all_to_all(copies, "path", 0, 0)


def split(value, terms):
    parts = []
    for _ in range(terms):
        part = value.astype(BF16)
        parts.append(part)
        value = value - part.astype(F32)
    return parts


def contract(lhs, rhs, lhs_dim, rhs_dim, precision=None):
    return lax.dot_general(
        lhs,
        rhs,
        (((lhs_dim,), (rhs_dim,)), ((), ())),
        precision=precision,
        preferred_element_type=F32,
    )


def folded(parts, rows):
    total = parts[:rows]
    for first in range(rows, parts.shape[0], rows):
        total = total + parts[first : first + rows]
    return total


def stack(value):
    return jnp.concatenate(split(value, 3), axis=0)


def each(count, body):
    def step(index, carry):
        body(index)
        return carry

    lax.fori_loop(0, count, step, 0)


def copy_of(source, target, sems, index):
    return pltpu.make_async_copy(source.at[index], target.at[index], sems.at[index])


def date_rows(date, knot_count):
    point = lax.broadcasted_iota(jnp.int32, (1, knot_count), 1) + 1
    alive = 120 * point > knot_count * (date + 1)
    maturity = HORIZON_YEARS * point.astype(F32) / knot_count
    fixing = STEP_YEARS * (date + 1).astype(F32)
    horizon = jnp.where(alive, maturity - fixing, 0.0)
    loading = (1.0 - jnp.exp(-MEAN_REV * horizon)) / MEAN_REV
    return alive, horizon, loading


def member_rows(flows, knot_count, set_count):
    digits = flows[:, knot_count : knot_count + 2].astype(F32)
    sets = (digits[:, 0:1] * BASE + digits[:, 1:2]).astype(jnp.int32)
    labels = lax.broadcasted_iota(jnp.int32, (flows.shape[0], set_count), 1)
    return sets == labels


def prep_kernel(end_ref, set_ref, cash_ref, out_ref):
    shards, trades, width = out_ref.shape
    knot_count = cash_ref.shape[1]
    row = lax.broadcasted_iota(jnp.int32, (trades, width), 0)
    point = lax.broadcasted_iota(jnp.int32, (trades, width), 1)
    ends = jnp.zeros((trades, width), jnp.int32)
    sets = jnp.zeros((trades, width), jnp.int32)
    for trade in range(trades):
        ends = jnp.where(row == trade, end_ref[trade], ends)
        sets = jnp.where(row == trade, set_ref[trade], sets)
    cash = jnp.concatenate(
        [cash_ref[...].astype(F32), jnp.zeros((trades, width - knot_count), F32)], axis=1
    )
    high = lax.shift_right_logical(sets, BASE.bit_length() - 1)
    low = sets & (BASE - 1)
    flows = jnp.where(point < jnp.minimum(ends, knot_count), cash, 0.0)
    flows = jnp.where(point == knot_count, high.astype(F32), flows)
    flows = jnp.where(point == knot_count + 1, low.astype(F32), flows).astype(BF16)
    for shard in range(shards):
        out_ref[shard] = flows


def curve_kernel(knots_ref, jac_ref, cpty_ref, prob_ref, rate_ref, weight_ref):
    knot_count = jac_ref.shape[0]
    column = jnp.sum(jac_ref[...] * knots_ref[...], axis=1, keepdims=True)
    rate_ref[...] = jnp.broadcast_to(column, (knot_count, LANES)).T[0:1]
    labels = lax.broadcasted_iota(jnp.int32, (prob_ref.shape[1], cpty_ref.shape[1]), 0)
    chosen = (cpty_ref[...] == labels).astype(F32)
    weight_ref[...] = LOSS_RATE * contract(prob_ref[...], chosen, 1, 0, HIGHEST)


def feature_kernel(
    vol_ref, normals_ref, start_ref, load_ref, rate_ref,
    exact_hbm, feat_hbm, exact_sum_ref, feat_sum_ref,
    exact_buf, feat_buf, exact_sems, feat_sems, state, stacked,
):
    dates = normals_ref.shape[0]
    knot_count = load_ref.shape[1]
    state[...] = start_ref[...]
    high, middle, low = split(load_ref[...], 3)
    stacked[...] = jnp.concatenate([high, middle, high, middle, low, high], axis=0)

    def one(date):
        now = DECAY * state[...] + vol_ref[date] * normals_ref[date]
        state[...] = now
        high, middle, low = split(now, 3)
        terms = jnp.concatenate([high, high, middle, middle, high, low], axis=0)
        alive, horizon, loading = date_rows(date, knot_count)
        discount = jnp.where(alive, jnp.exp(-rate_ref[...] * horizon), 0.0)
        shift = contract(terms, stacked[...], 0, 0)
        exact = discount * jnp.exp(-loading * shift)
        exact_buf[date] = exact
        rounded = exact.astype(BF16)
        feat_buf[date] = rounded
        copy_of(exact_buf, exact_hbm, exact_sems, date).start()
        copy_of(feat_buf, feat_hbm, feat_sems, date).start()
        row = pl.ds(date, 1)
        exact_sum_ref[row, :] = jnp.sum(exact, axis=0, keepdims=True)
        feat_sum_ref[row, :] = jnp.sum(rounded.astype(F32), axis=0, keepdims=True)

    each(dates, one)
    each(dates, lambda date: copy_of(exact_buf, exact_hbm, exact_sems, date).wait())
    each(dates, lambda date: copy_of(feat_buf, feat_hbm, feat_sems, date).wait())


def net_kernel(flows_ref, feat_sum_ref, net_ref, out_ref):
    knot_count, sets = net_ref.shape
    flows = flows_ref[...]
    member = member_rows(flows, knot_count, sets).astype(BF16)
    net = contract(flows[:, :knot_count], member, 0, 0).astype(BF16)
    net_ref[...] = net
    sums = folded(contract(stack(feat_sum_ref[...]), net, 1, 0), out_ref.shape[1])
    out_ref[...] = jnp.broadcast_to(sums[None], out_ref.shape)


def value_kernel(flows_ref, net_ref, feat_hbm, values_ref, rows_ref, feat_buf, sems):
    dates = values_ref.shape[0]
    each(dates, lambda date: copy_of(feat_hbm, feat_buf, sems, date).start())
    sets, knot_count = rows_ref.shape
    flows = flows_ref[...]
    member = member_rows(flows, knot_count, sets).astype(BF16)
    rows_ref[...] = contract(member, flows[:, :knot_count], 0, 0).astype(BF16)

    def one(date):
        copy_of(feat_hbm, feat_buf, sems, date).wait()
        values_ref[date] = contract(feat_buf[date], net_ref[...], 1, 0)

    each(dates, one)


def slope_of(values, mean, base, weight):
    return weight * jax.nn.sigmoid(SHARPNESS * (values - mean + base))


def slope_kernel(paths, arrived_ref, values_ref, weight_ref, base_ref, mean_ref, sums_ref, out_ref):
    mean_ref[...] = jnp.sum(arrived_ref[...], axis=0) / paths
    for date in range(values_ref.shape[0]):
        row = slice(date, date + 1)
        slope = slope_of(values_ref[date], mean_ref[row, :], base_ref[row, :], weight_ref[row, :])
        sums_ref[row, :] = jnp.sum(slope, axis=0, keepdims=True)
    out_ref[...] = jnp.broadcast_to(sums_ref[...][None], out_ref.shape)


def adjoint_kernel(
    mean_ref, sums_ref, weight_ref, base_ref, feat_sum_ref, values_ref, net_ref, flows_ref, exact_hbm,
    blend_ref, rate_ref, trades_ref, cross_ref, exact_buf, sems, rate, loads,
):
    dates = values_ref.shape[0]
    paths, knot_count = blend_ref.shape
    each(dates, lambda date: copy_of(exact_hbm, exact_buf, sems, date).start())
    blend_ref[...] = jnp.zeros_like(blend_ref)
    rate[...] = jnp.zeros_like(rate)
    loads[...] = jnp.zeros_like(loads)
    flows = flows_ref[...]
    member = member_rows(flows, knot_count, net_ref.shape[0])
    flows = flows[:, :knot_count]
    cross_ref[...] = folded(contract(stack(feat_sum_ref[...]), flows, 1, 1), dates)

    def one(date):
        _, horizon, loading = date_rows(date, knot_count)
        factor = loading * jnp.exp(-MEAN_REV * STEP_YEARS * (date + 1).astype(F32))
        row = pl.ds(date, 1)
        slope = slope_of(values_ref[date], mean_ref[row, :], base_ref[row, :], weight_ref[row, :])
        adjoint = (slope - sums_ref[row, :] / paths).astype(BF16)
        copy_of(exact_hbm, exact_buf, sems, date).wait()
        exact = exact_buf[date]
        product = contract(adjoint, net_ref[...], 1, 0) * exact
        blend_ref[...] += factor * product
        rate[...] += horizon * jnp.sum(product.reshape(-1, 8, knot_count), axis=0)
        loads[...] += contract(adjoint, exact.astype(BF16), 0, 0)

    each(dates, one)
    shares = jnp.zeros(member.shape, F32)
    for part in split(loads[...], 3):
        shares = shares + contract(flows, part, 1, 1)
    trades_ref[...] = jnp.sum(jnp.where(member, shares, 0.0).T, axis=0, keepdims=True)
    rate_ref[...] = jnp.sum(rate[...], axis=0, keepdims=True)


def finish_kernel(
    paths, local, arrived_ref, sums_ref, exact_sum_ref, net_ref, flows_ref, rate_ref, trades_ref, cross_ref,
    shift_ref, out_ref,
):
    sets, knot_count = net_ref.shape
    gap = sums_ref[...] / local - jnp.sum(arrived_ref[...], axis=0) / paths
    flows = flows_ref[...]
    member = member_rows(flows, knot_count, sets).astype(BF16)
    terms = stack(gap)
    spread = folded(contract(terms, member, 1, 1), gap.shape[0])
    adjoint = folded(contract(terms, net_ref[...], 1, 0), gap.shape[0])
    total = rate_ref[...]
    for date in range(shift_ref.shape[0]):
        row = slice(date, date + 1)
        _, horizon, loading = date_rows(jnp.int32(date), knot_count)
        shift_ref[row, :] = loading * math.exp(-MEAN_REV * STEP_YEARS * (date + 1)) * adjoint[row]
        total = total + horizon * adjoint[row] * exact_sum_ref[row, :]
    trades = trades_ref[...] + jnp.sum(spread * cross_ref[...], axis=0, keepdims=True)
    shards, _, width = out_ref.shape
    pad = jnp.zeros((1, width - knot_count - trades.shape[1]), F32)
    row = jnp.concatenate([-total / paths, pad, trades / paths], axis=1)
    out_ref[...] = jnp.broadcast_to(row[None], out_ref.shape)


def start_kernel(blend_ref, shift_ref, load_ref, later_ref, exact_hbm, out_ref, exact_buf, sems, blend):
    dates = shift_ref.shape[0]
    each(dates, lambda date: copy_of(exact_hbm, exact_buf, sems, date).start())
    blend[...] = blend_ref[...]

    def one(date):
        copy_of(exact_hbm, exact_buf, sems, date).wait()
        blend[...] += shift_ref[pl.ds(date, 1), :] * exact_buf[date]

    each(dates, one)
    carried = contract(load_ref[...], blend[...], 1, 1, HIGHEST)
    out_ref[...] = math.exp(-MEAN_REV * STEP_YEARS * dates) * later_ref[...] - carried


def final_kernel(index_ref, arrived_ref, jac_hbm, knot_ref, alloc_ref, jac_buf, sems, column, total):
    blocks, rows, knot_count = jac_hbm.shape
    each(blocks, lambda block: copy_of(jac_hbm, jac_buf, sems, block).start())
    row = jnp.sum(arrived_ref[...], axis=0)
    trades = alloc_ref.shape[1]
    parts = row[:, round_up(knot_count, LANES) :]
    count = parts.shape[1]
    offset = index_ref[0] * trades
    parts = jnp.broadcast_to(parts, (8, count))
    alloc_ref[...] = pltpu.roll(parts, lax.rem(count - offset, count), 1)[0:1, :trades]
    column[...] = jnp.broadcast_to(row[:, :knot_count], (LANES, knot_count)).T
    total[...] = jnp.zeros_like(total)

    def one(block):
        copy_of(jac_hbm, jac_buf, sems, block).wait()
        part = column[pl.ds(pl.multiple_of(block * rows, rows), rows), :]
        for first in range(0, knot_count, LANES):
            size = min(LANES, knot_count - first)
            cut = slice(first, first + size)
            scaled = jac_buf[block, :, cut] * part[:, :size]
            total[:, cut] += jnp.sum(scaled.reshape(-1, total.shape[0], size), axis=0)

    each(blocks, one)
    knot_ref[...] = jnp.sum(total[...], axis=0, keepdims=True)


VMEM = pl.BlockSpec(memory_space=pltpu.VMEM)
SMEM = pl.BlockSpec(memory_space=pltpu.SMEM)


def shaped(shape, dtype=F32):
    return jax.ShapeDtypeStruct(shape, dtype)


def held(array):
    size = array.dtype.itemsize
    rows = array.shape[-2] if len(array.shape) > 1 else 1
    lead = math.prod(array.shape[:-2])
    return lead * round_up(rows, 8) * round_up(array.shape[-1], LANES) * size


def run(name, kernel, out_shape, operands, scalars=0, hbm=(), scratch=(), copies=(), flops=0, grant=0):
    arrays = list(operands) + list(out_shape)
    room = sum(held(array) for array in scratch) + (8 << 20)
    specs = []
    for place, array in enumerate(arrays):
        if place < scalars:
            specs.append(SMEM)
        elif place in hbm:
            specs.append(pl.BlockSpec(memory_space=pltpu.HBM))
        else:
            specs.append(VMEM)
            room += held(array)
    moved = sum(held(array) for array in arrays)
    return pl.pallas_call(
        kernel,
        out_shape=tuple(out_shape),
        in_specs=specs[: len(operands)],
        out_specs=tuple(specs[len(operands) :]),
        scratch_shapes=[pltpu.VMEM(array.shape, array.dtype) for array in scratch[: len(copies)]]
        + [pltpu.SemaphoreType.DMA((count,)) for count in copies]
        + [pltpu.VMEM(array.shape, array.dtype) for array in scratch[len(copies) :]],
        compiler_params=pltpu.CompilerParams(vmem_limit_bytes=grant or room),
        cost_estimate=pl.CostEstimate(flops=flops, bytes_accessed=moved, transcendentals=0),
        name=name,
    )(*operands)


def per_device(
    normals,
    start_state,
    later_adjoint,
    vol,
    factor_load,
    knots,
    spline_jac,
    cashflows,
    trade_set,
    trade_end,
    set_cpty,
    default_prob,
    base_value,
):
    dates, factors, paths = normals.shape
    knot_count = knots.shape[0]
    sets = base_value.shape[1]
    shards = lax.axis_size("path")
    trades = cashflows.shape[0]
    all_trades = trades * shards
    all_paths = paths * shards
    width = round_up(knot_count + 2, LANES)
    work = 2 * dates * paths * knot_count
    grid_rows = shaped((dates, knot_count))
    set_rows = shaped((dates, sets))
    set_copies = shaped((shards, dates, sets))

    (copies,) = run(
        "prep",
        prep_kernel,
        [shaped((shards, trades, width), BF16)],
        [trade_end, trade_set.reshape(trades), cashflows],
        scalars=2,
        grant=LARGE,
    )
    arrived = exchange(copies)

    zero_rate, weight = run(
        "curve",
        curve_kernel,
        [shaped((1, knot_count)), set_rows],
        [knots.reshape(1, knot_count), spline_jac, set_cpty.reshape(1, sets), default_prob],
        flops=2 * knot_count**2,
        grant=LARGE,
    )
    exact, features, exact_sums, feat_sums = run(
        "features",
        feature_kernel,
        [
            shaped((dates, paths, knot_count)),
            shaped((dates, paths, knot_count), BF16),
            grid_rows,
            grid_rows,
        ],
        [vol, normals, start_state, factor_load, zero_rate],
        scalars=1,
        hbm=(5, 6),
        scratch=[
            shaped((dates, paths, knot_count)),
            shaped((dates, paths, knot_count), BF16),
            shaped((factors, paths)),
            shaped((6 * factors, knot_count), BF16),
        ],
        copies=(dates, dates),
        flops=6 * factors * work,
        grant=MIDDLE,
    )

    flows = arrived.reshape(all_trades, width)
    net_columns, copies = run(
        "net",
        net_kernel,
        [shaped((knot_count, sets), BF16), set_copies],
        [flows, feat_sums],
        flops=2 * sets * all_trades * knot_count,
    )
    arrived = exchange(copies)
    values, net_rows = run(
        "values",
        value_kernel,
        [shaped((dates, paths, sets)), shaped((sets, knot_count), BF16)],
        [flows, net_columns, features],
        hbm=(2,),
        scratch=[shaped((dates, paths, knot_count), BF16)],
        copies=(dates,),
        flops=sets * work,
        grant=MIDDLE,
    )
    mean, slope_sums, copies = run(
        "slopes",
        functools.partial(slope_kernel, all_paths),
        [set_rows, set_rows, set_copies],
        [arrived, values, weight, base_value],
        flops=16 * dates * paths * sets,
    )
    arrived = exchange(copies)
    blend, rate, trade_parts, cross = run(
        "adjoint",
        adjoint_kernel,
        [
            shaped((paths, knot_count)),
            shaped((1, knot_count)),
            shaped((1, all_trades)),
            shaped((dates, all_trades)),
        ],
        [mean, slope_sums, weight, base_value, feat_sums, values, net_rows, flows, exact],
        hbm=(8,),
        scratch=[
            shaped((dates, paths, knot_count)),
            shaped((8, knot_count)),
            shaped((sets, knot_count)),
        ],
        copies=(dates,),
        flops=2 * sets * work,
        grant=MIDDLE,
    )
    row_width = round_up(knot_count, LANES) + all_trades
    shift, copies = run(
        "finish",
        functools.partial(finish_kernel, all_paths, paths),
        [grid_rows, shaped((shards, 1, row_width))],
        [arrived, slope_sums, exact_sums, net_rows, flows, rate, trade_parts, cross],
        flops=6 * sets * dates * knot_count,
    )
    arrived = exchange(copies)
    (start_adjoint,) = run(
        "start",
        start_kernel,
        [shaped((factors, paths))],
        [blend, shift, factor_load, later_adjoint, exact],
        hbm=(4,),
        scratch=[shaped((dates, paths, knot_count)), shaped((paths, knot_count))],
        copies=(dates,),
        flops=2 * factors * paths * knot_count,
        grant=MIDDLE,
    )
    blocks = next(count for count in (8, 4, 2, 1) if knot_count % (8 * count) == 0)
    index = lax.axis_index("path").astype(jnp.int32).reshape(1)
    knot_grad, alloc = run(
        "final",
        final_kernel,
        [shaped((1, knot_count)), shaped((1, trades))],
        [index, arrived, spline_jac.reshape(blocks, knot_count // blocks, knot_count)],
        scalars=1,
        hbm=(2,),
        scratch=[
            shaped((blocks, knot_count // blocks, knot_count)),
            shaped((knot_count, LANES)),
            shaped((8, knot_count)),
        ],
        copies=(blocks,),
        flops=2 * knot_count**2,
        grant=52 << 20,
    )
    return knot_grad.reshape(knot_count), alloc.reshape(trades), start_adjoint


def solution(mesh):
    in_specs = (
        P(None, None, ("group", "path")),
        P(None, ("group", "path")),
        P(None, ("group", "path")),
        P(),
        P(),
        P(),
        P(),
        P(("group", "path"), None),
        P(("group", "path"), None),
        P(("group", "path")),
        P("group", None),
        P(),
        P(None, "group"),
    )
    out_specs = (P("group"), P(("group", "path")), P(None, ("group", "path")))
    return jax.shard_map(
        per_device, mesh=mesh, in_specs=in_specs, out_specs=out_specs, check_vma=False
    )
```

```python
import functools
import math

import jax
import jax.numpy as jnp
from jax import lax
from jax.experimental import pallas as pl
from jax.experimental.pallas import tpu as pltpu
from jax.sharding import PartitionSpec as P

MEAN_REV = 0.05
STEP_YEARS = 0.25
HORIZON_YEARS = 30.0
SHARPNESS = 4.0
LOSS_RATE = 0.6
BASE = 128
LANES = 128
LARGE = 58 << 20
MIDDLE = 50 << 20
LOG2E = math.log2(math.e)
DECAY = math.exp(-MEAN_REV * STEP_YEARS)
HIGHEST = lax.Precision.HIGHEST
F32 = jnp.float32
BF16 = jnp.bfloat16


def round_up(size, step):
    return -(-size // step) * step


def exchange(copies, groups=None):
    return lax.all_to_all(copies, "path", 0, 0, axis_index_groups=groups)


def split(value, terms):
    parts = []
    for _ in range(terms):
        part = value.astype(BF16)
        parts.append(part)
        value = value - part.astype(F32)
    return parts


def contract(lhs, rhs, lhs_dim, rhs_dim, precision=None):
    return lax.dot_general(
        lhs,
        rhs,
        (((lhs_dim,), (rhs_dim,)), ((), ())),
        precision=precision,
        preferred_element_type=F32,
    )


def folded(parts, rows):
    total = parts[:rows]
    for first in range(rows, parts.shape[0], rows):
        total = total + parts[first : first + rows]
    return total


def stack(value):
    return jnp.concatenate(split(value, 3), axis=0)


def each(count, body, group=1):
    def step(index, carry):
        for offset in range(group):
            body(index * group + offset)
        return carry

    lax.fori_loop(0, count // group, step, 0)


def copy_of(source, target, sems, index):
    return pltpu.make_async_copy(source.at[index], target.at[index], sems.at[index])


def date_rows(date, knot_count):
    point = lax.broadcasted_iota(jnp.int32, (1, knot_count), 1) + 1
    alive = 120 * point > knot_count * (date + 1)
    maturity = HORIZON_YEARS * point.astype(F32) / knot_count
    fixing = STEP_YEARS * (date + 1).astype(F32)
    horizon = jnp.where(alive, maturity - fixing, 0.0)
    loading = (1.0 - jnp.exp(-MEAN_REV * horizon)) / MEAN_REV
    return alive, horizon, loading


def member_rows(flows, knot_count, set_count):
    digits = flows[:, knot_count : knot_count + 2].astype(F32)
    sets = (digits[:, 0:1] * BASE + digits[:, 1:2]).astype(jnp.int32)
    labels = lax.broadcasted_iota(jnp.int32, (flows.shape[0], set_count), 1)
    return sets == labels


def prep_kernel(end_ref, set_ref, cash_ref, out_ref):
    shards, trades, width = out_ref.shape
    knot_count = cash_ref.shape[1]
    row = lax.broadcasted_iota(jnp.int32, (trades, width), 0)
    point = lax.broadcasted_iota(jnp.int32, (trades, width), 1)
    ends = jnp.zeros((trades, width), jnp.int32)
    sets = jnp.zeros((trades, width), jnp.int32)
    for trade in range(trades):
        ends = jnp.where(row == trade, end_ref[trade], ends)
        sets = jnp.where(row == trade, set_ref[trade], sets)
    cash = jnp.concatenate(
        [cash_ref[...].astype(F32), jnp.zeros((trades, width - knot_count), F32)], axis=1
    )
    high = lax.shift_right_logical(sets, BASE.bit_length() - 1)
    low = sets & (BASE - 1)
    flows = jnp.where(point < jnp.minimum(ends, knot_count), cash, 0.0)
    flows = jnp.where(point == knot_count, high.astype(F32), flows)
    flows = jnp.where(point == knot_count + 1, low.astype(F32), flows).astype(BF16)
    for shard in range(shards):
        out_ref[shard] = flows


def feature_kernel(
    vol_hbm, normals_hbm, start_hbm, load_hbm, knots_hbm, jac_hbm,
    exact_hbm, feat_sum_ref,
    exact_buf, jac_buf, exact_sems, jac_sems, sems, normals_ref, state, load_ref, knots_ref, stacked, column, rate_ref, vol_ref,
):
    dates = normals_ref.shape[0]
    blocks, rows, knot_count = jac_hbm.shape
    inputs = [
        pltpu.make_async_copy(source, target, sems.at[place])
        for place, (source, target) in enumerate(
            ((load_hbm, load_ref), (knots_hbm, knots_ref), (start_hbm, state), (normals_hbm, normals_ref), (vol_hbm, vol_ref))
        )
    ]
    for copy in inputs:
        copy.start()
    each(blocks, lambda block: copy_of(jac_hbm, jac_buf, jac_sems, block).start())
    inputs[0].wait()
    high, middle, low = split(load_ref[...], 3)
    stacked[...] = jnp.concatenate([high, middle, high, middle, low, high], axis=0)
    for copy in inputs[1:]:
        copy.wait()

    parts = exact_sems.shape[0] // dates
    size = exact_buf.shape[1] // parts

    def sent(date, part):
        cut = pl.ds(part * size, size)
        sem = exact_sems.at[date * parts + part]
        return pltpu.make_async_copy(exact_buf.at[date, cut], exact_hbm.at[date, cut], sem)

    def zero_rates(block):
        copy_of(jac_hbm, jac_buf, jac_sems, block).wait()
        sums = jnp.sum(jac_buf[block] * knots_ref[...], axis=1, keepdims=True)
        column[pl.ds(pl.multiple_of(block * rows, rows), rows), :] = jnp.broadcast_to(sums, (rows, LANES))

    each(blocks, zero_rates)
    rate_ref[...] = column[...].T[0:1]

    def one(date):
        now = DECAY * state[...] + vol_ref[date] * normals_ref[date]
        state[...] = now
        high, middle, low = split(now, 3)
        terms = jnp.concatenate([high, high, middle, middle, high, low], axis=0)
        alive, horizon, loading = date_rows(date, knot_count)
        discount = jnp.where(alive, jnp.exp(-rate_ref[...] * horizon), 0.0)
        shift = contract(terms, stacked[...], 0, 0)
        exact = discount * jnp.exp2((-LOG2E * loading) * shift)
        exact_buf[date] = exact
        for part in range(parts):
            sent(date, part).start()
        row = pl.ds(date, 1)
        ones = jnp.ones((8, exact.shape[0]), BF16)
        feat_sum_ref[row, :] = contract(ones, exact.astype(BF16), 1, 0)[0:1]

    each(dates, one, 8)
    for part in range(parts):
        each(dates, lambda date, part=part: sent(date, part).wait())


def half_kernel(own_ref, feat_sum_ref, half_ref, terms_ref):
    knot_count, sets = half_ref.shape
    flows = own_ref[...]
    member = member_rows(flows, knot_count, sets).astype(BF16)
    half_ref[...] = contract(flows[:, :knot_count], member, 0, 0)
    terms_ref[...] = stack(feat_sum_ref[...])


def net_kernel(own_ref, other_ref, half_ref, terms_ref, flows_ref, net_ref, out_ref):
    knot_count, sets = net_ref.shape
    flows_ref[...] = jnp.concatenate([own_ref[...], other_ref[...]], axis=0)
    flows = other_ref[...]
    member = member_rows(flows, knot_count, sets).astype(BF16)
    net = (half_ref[...] + contract(flows[:, :knot_count], member, 0, 0)).astype(BF16)
    net_ref[...] = net
    sums = folded(contract(terms_ref[...], net, 1, 0), out_ref.shape[1])
    out_ref[...] = jnp.broadcast_to(sums[None], out_ref.shape)


def value_kernel(
    flows_ref, net_ref, cpty_ref, prob_ref, exact_hbm, values_ref, rows_ref, weight_ref, exact_buf, sems
):
    dates = values_ref.shape[0]
    each(dates, lambda date: copy_of(exact_hbm, exact_buf, sems, date).start())
    labels = lax.broadcasted_iota(jnp.int32, (prob_ref.shape[1], cpty_ref.shape[1]), 0)
    chosen = (cpty_ref[...] == labels).astype(F32)
    weight_ref[...] = LOSS_RATE * contract(prob_ref[...], chosen, 1, 0, HIGHEST)
    sets, knot_count = rows_ref.shape
    half = flows_ref.shape[0] // 2
    rows = []
    for first in (0, half):
        flows = flows_ref[first : first + half, :]
        member = member_rows(flows, knot_count, sets).astype(BF16)
        rows.append(contract(member, flows[:, :knot_count], 0, 0))
    rows_ref[...] = (rows[0] + rows[1]).astype(BF16)

    def one(date):
        copy_of(exact_hbm, exact_buf, sems, date).wait()
        values_ref[date] = contract(exact_buf[date].astype(BF16), net_ref[...], 1, 0)

    each(dates, one)


def slope_of(values, mean, base, weight):
    return weight * jax.nn.sigmoid(SHARPNESS * (values - mean + base))


def slope_kernel(paths, arrived_ref, values_ref, weight_ref, base_ref, mean_ref, sums_ref, out_ref):
    mean_ref[...] = jnp.sum(arrived_ref[...], axis=0) / paths
    for date in range(values_ref.shape[0]):
        row = slice(date, date + 1)
        slope = slope_of(values_ref[date], mean_ref[row, :], base_ref[row, :], weight_ref[row, :])
        sums_ref[row, :] = jnp.sum(slope, axis=0, keepdims=True)
    out_ref[...] = jnp.broadcast_to(sums_ref[...][None], out_ref.shape)


def adjoint_kernel(
    mean_ref, sums_ref, weight_ref, base_ref, feat_sum_ref, values_ref, net_ref, flows_ref, exact_hbm,
    blend_ref, rate_ref, trades_ref, cross_ref, exact_buf, sems, rate, loads,
):
    dates = values_ref.shape[0]
    paths, knot_count = blend_ref.shape
    each(dates, lambda date: copy_of(exact_hbm, exact_buf, sems, date).start())
    blend_ref[...] = jnp.zeros_like(blend_ref)
    rate[...] = jnp.zeros_like(rate)
    loads[...] = jnp.zeros_like(loads)
    flows = flows_ref[...]
    member = member_rows(flows, knot_count, net_ref.shape[0])
    flows = flows[:, :knot_count]
    cross_ref[...] = folded(contract(stack(feat_sum_ref[...]), flows, 1, 1), dates)

    def one(date):
        _, horizon, loading = date_rows(date, knot_count)
        factor = loading * jnp.exp(-MEAN_REV * STEP_YEARS * (date + 1).astype(F32))
        row = pl.ds(date, 1)
        slope = slope_of(values_ref[date], mean_ref[row, :], base_ref[row, :], weight_ref[row, :])
        adjoint = (slope - sums_ref[row, :] / paths).astype(BF16)
        copy_of(exact_hbm, exact_buf, sems, date).wait()
        exact = exact_buf[date]
        product = contract(adjoint, net_ref[...], 1, 0) * exact
        blend_ref[...] += factor * product
        rate[...] += horizon * jnp.sum(product.reshape(-1, 8, knot_count), axis=0)
        loads[...] += contract(adjoint, exact.astype(BF16), 0, 0)

    each(dates, one)
    shares = jnp.zeros(member.shape, F32)
    for part in split(loads[...], 3):
        shares = shares + contract(flows, part, 1, 1)
    trades_ref[...] = jnp.sum(jnp.where(member, shares, 0.0).T, axis=0, keepdims=True)
    rate_ref[...] = jnp.sum(rate[...], axis=0, keepdims=True)


def finish_kernel(
    paths, local, parity_ref, arrived_ref, sums_ref, feat_sum_ref, net_ref, flows_ref, rate_ref, trades_ref, cross_ref,
    shift_ref, out_ref,
):
    sets, knot_count = net_ref.shape
    gap = sums_ref[...] / local - jnp.sum(arrived_ref[...], axis=0) / paths
    flows = flows_ref[...]
    member = member_rows(flows, knot_count, sets).astype(BF16)
    terms = stack(gap)
    spread = folded(contract(terms, member, 1, 1), gap.shape[0])
    adjoint = folded(contract(terms, net_ref[...], 1, 0), gap.shape[0])
    total = rate_ref[...]
    for date in range(shift_ref.shape[0]):
        row = slice(date, date + 1)
        _, horizon, loading = date_rows(jnp.int32(date), knot_count)
        shift_ref[row, :] = loading * math.exp(-MEAN_REV * STEP_YEARS * (date + 1)) * adjoint[row]
        total = total + horizon * adjoint[row] * feat_sum_ref[row, :]
    trades = trades_ref[...] + jnp.sum(spread * cross_ref[...], axis=0, keepdims=True)
    count = trades.shape[1]
    trades = pltpu.roll(jnp.broadcast_to(trades, (8, count)), parity_ref[0] * (count // 2), 1)[0:1]
    shards, _, width = out_ref.shape
    pad = jnp.zeros((1, width - knot_count - trades.shape[1]), F32)
    row = jnp.concatenate([-total / paths, pad, trades / paths], axis=1)
    out_ref[...] = jnp.broadcast_to(row[None], out_ref.shape)


def start_kernel(blend_ref, shift_ref, load_ref, later_ref, exact_hbm, out_ref, exact_buf, sems, blend):
    dates = shift_ref.shape[0]
    each(dates, lambda date: copy_of(exact_hbm, exact_buf, sems, date).start())
    blend[...] = blend_ref[...]

    def one(date):
        copy_of(exact_hbm, exact_buf, sems, date).wait()
        blend[...] += shift_ref[pl.ds(date, 1), :] * exact_buf[date]

    each(dates, one)
    carried = contract(load_ref[...], blend[...], 1, 1, HIGHEST)
    out_ref[...] = math.exp(-MEAN_REV * STEP_YEARS * dates) * later_ref[...] - carried


def final_kernel(index_ref, arrived_ref, jac_hbm, knot_ref, alloc_ref, jac_buf, sems, column, total):
    blocks, rows, knot_count = jac_hbm.shape
    each(blocks, lambda block: copy_of(jac_hbm, jac_buf, sems, block).start())
    row = jnp.sum(arrived_ref[...], axis=0)
    trades = alloc_ref.shape[1]
    parts = row[:, round_up(knot_count, LANES) :]
    count = parts.shape[1]
    offset = index_ref[0]
    parts = jnp.broadcast_to(parts, (8, count))
    alloc_ref[...] = pltpu.roll(parts, lax.rem(count - offset, count), 1)[0:1, :trades]
    column[...] = jnp.broadcast_to(row[:, :knot_count], (LANES, knot_count)).T
    total[...] = jnp.zeros_like(total)

    def one(block):
        copy_of(jac_hbm, jac_buf, sems, block).wait()
        part = column[pl.ds(pl.multiple_of(block * rows, rows), rows), :]
        for first in range(0, knot_count, LANES):
            size = min(LANES, knot_count - first)
            cut = slice(first, first + size)
            scaled = jac_buf[block, :, cut] * part[:, :size]
            total[:, cut] += jnp.sum(scaled.reshape(-1, total.shape[0], size), axis=0)

    each(blocks, one)
    knot_ref[...] = jnp.sum(total[...], axis=0, keepdims=True)


VMEM = pl.BlockSpec(memory_space=pltpu.VMEM)
SMEM = pl.BlockSpec(memory_space=pltpu.SMEM)


def shaped(shape, dtype=F32):
    return jax.ShapeDtypeStruct(shape, dtype)


def held(array):
    size = array.dtype.itemsize
    rows = array.shape[-2] if len(array.shape) > 1 else 1
    lead = math.prod(array.shape[:-2])
    return lead * round_up(rows, 8) * round_up(array.shape[-1], LANES) * size


def run(name, kernel, out_shape, operands, scalars=0, hbm=(), scratch=(), copies=(), buffers=1, smem=(), flops=0, grant=0):
    arrays = list(operands) + list(out_shape)
    room = sum(held(array) for array in scratch) + (8 << 20)
    specs = []
    for place, array in enumerate(arrays):
        if place < scalars:
            specs.append(SMEM)
        elif place in hbm:
            specs.append(pl.BlockSpec(memory_space=pltpu.HBM))
        else:
            specs.append(VMEM)
            room += held(array)
    moved = sum(held(array) for array in arrays)
    return pl.pallas_call(
        kernel,
        out_shape=tuple(out_shape),
        in_specs=specs[: len(operands)],
        out_specs=tuple(specs[len(operands) :]),
        scratch_shapes=[pltpu.VMEM(array.shape, array.dtype) for array in scratch[:buffers]]
        + [pltpu.SemaphoreType.DMA((count,)) for count in copies]
        + [pltpu.VMEM(array.shape, array.dtype) for array in scratch[buffers:]]
        + [pltpu.SMEM(array.shape, array.dtype) for array in smem],
        compiler_params=pltpu.CompilerParams(vmem_limit_bytes=grant or room),
        cost_estimate=pl.CostEstimate(flops=flops, bytes_accessed=moved, transcendentals=0),
        name=name,
    )(*operands)


def per_device(
    normals,
    start_state,
    later_adjoint,
    vol,
    factor_load,
    knots,
    spline_jac,
    cashflows,
    trade_set,
    trade_end,
    set_cpty,
    default_prob,
    base_value,
):
    dates, factors, paths = normals.shape
    knot_count = knots.shape[0]
    sets = base_value.shape[1]
    shards = lax.axis_size("path")
    trades = cashflows.shape[0]
    all_trades = trades * shards
    all_paths = paths * shards
    width = round_up(knot_count + 2, LANES)
    work = 2 * dates * paths * knot_count
    grid_rows = shaped((dates, knot_count))
    set_rows = shaped((dates, sets))
    set_copies = shaped((shards, dates, sets))

    (copies,) = run(
        "prep",
        prep_kernel,
        [shaped((shards // 2, trades, width), BF16)],
        [trade_end, trade_set.reshape(trades), cashflows],
        scalars=2,
        grant=LARGE,
    )
    own = exchange(copies, [list(range(side, shards, 2)) for side in range(2)])
    own = own.reshape(all_trades // 2, width)
    index = lax.axis_index("path").astype(jnp.int32)
    parity = lax.rem(index, 2)
    offset = parity * (all_trades // 2) + lax.div(index, 2) * trades
    blocks = next(count for count in (8, 4, 2, 1) if knot_count % (8 * count) == 0)
    jac_blocks = spline_jac.reshape(blocks, knot_count // blocks, knot_count)

    exact, feat_sums = run(
        "features",
        feature_kernel,
        [shaped((dates, paths, knot_count)), grid_rows],
        [vol, normals, start_state, factor_load, knots.reshape(1, knot_count), jac_blocks],
        hbm=(0, 1, 2, 3, 4, 5, 6),
        scratch=[
            shaped((dates, paths, knot_count)),
            shaped(jac_blocks.shape),
            shaped(normals.shape),
            shaped(start_state.shape),
            shaped(factor_load.shape),
            shaped((1, knot_count)),
            shaped((6 * factors, knot_count), BF16),
            shaped((knot_count, LANES)),
            shaped((1, knot_count)),
        ],
        buffers=2,
        copies=(dates * (4 if paths % 64 == 0 else 1), blocks, 5),
        smem=(shaped(vol.shape),),
        flops=6 * factors * work,
        grant=LARGE,
    )

    own, feat_sums = lax.optimization_barrier((own, feat_sums))
    other = lax.ppermute(own, "path", [(shard, shard ^ 1) for shard in range(shards)])
    half, terms = run(
        "half",
        half_kernel,
        [shaped((knot_count, sets)), shaped((3 * dates, knot_count), BF16)],
        [own, feat_sums],
        flops=sets * all_trades * knot_count,
    )
    flows, net_columns, copies = run(
        "net",
        net_kernel,
        [shaped((all_trades, width), BF16), shaped((knot_count, sets), BF16), set_copies],
        [own, other, half, terms],
        flops=sets * all_trades * knot_count,
    )
    arrived = exchange(copies)
    values, net_rows, weight = run(
        "values",
        value_kernel,
        [shaped((dates, paths, sets)), shaped((sets, knot_count), BF16), set_rows],
        [flows, net_columns, set_cpty.reshape(1, sets), default_prob, exact],
        hbm=(4,),
        scratch=[shaped((dates, paths, knot_count))],
        copies=(dates,),
        flops=sets * work,
        grant=MIDDLE,
    )
    mean, slope_sums, copies = run(
        "slopes",
        functools.partial(slope_kernel, all_paths),
        [set_rows, set_rows, set_copies],
        [arrived, values, weight, base_value],
        flops=16 * dates * paths * sets,
    )
    arrived = exchange(copies)
    blend, rate, trade_parts, cross = run(
        "adjoint",
        adjoint_kernel,
        [
            shaped((paths, knot_count)),
            shaped((1, knot_count)),
            shaped((1, all_trades)),
            shaped((dates, all_trades)),
        ],
        [mean, slope_sums, weight, base_value, feat_sums, values, net_rows, flows, exact],
        hbm=(8,),
        scratch=[
            shaped((dates, paths, knot_count)),
            shaped((8, knot_count)),
            shaped((sets, knot_count)),
        ],
        copies=(dates,),
        flops=2 * sets * work,
        grant=MIDDLE,
    )
    row_width = round_up(knot_count, LANES) + all_trades
    shift, copies = run(
        "finish",
        functools.partial(finish_kernel, all_paths, paths),
        [grid_rows, shaped((shards, 1, row_width))],
        [parity.reshape(1), arrived, slope_sums, feat_sums, net_rows, flows, rate, trade_parts, cross],
        scalars=1,
        flops=6 * sets * dates * knot_count,
    )
    arrived = exchange(copies)
    (start_adjoint,) = run(
        "start",
        start_kernel,
        [shaped((factors, paths))],
        [blend, shift, factor_load, later_adjoint, exact],
        hbm=(4,),
        scratch=[shaped((dates, paths, knot_count)), shaped((paths, knot_count))],
        copies=(dates,),
        flops=2 * factors * paths * knot_count,
        grant=MIDDLE,
    )
    knot_grad, alloc = run(
        "final",
        final_kernel,
        [shaped((1, knot_count)), shaped((1, trades))],
        [offset.reshape(1), arrived, jac_blocks],
        scalars=1,
        hbm=(2,),
        scratch=[
            shaped(jac_blocks.shape),
            shaped((knot_count, LANES)),
            shaped((8, knot_count)),
        ],
        copies=(blocks,),
        flops=2 * knot_count**2,
        grant=52 << 20,
    )
    return knot_grad.reshape(knot_count), alloc.reshape(trades), start_adjoint


def solution(mesh):
    in_specs = (
        P(None, None, ("group", "path")),
        P(None, ("group", "path")),
        P(None, ("group", "path")),
        P(),
        P(),
        P(),
        P(),
        P(("group", "path"), None),
        P(("group", "path"), None),
        P(("group", "path")),
        P("group", None),
        P(),
        P(None, "group"),
    )
    out_specs = (P("group"), P(("group", "path")), P(None, ("group", "path")))
    return jax.shard_map(
        per_device, mesh=mesh, in_specs=in_specs, out_specs=out_specs, check_vma=False
    )
```

```python
import functools
import math

import jax
import jax.numpy as jnp
from jax import lax
from jax.experimental import pallas as pl
from jax.experimental.pallas import tpu as pltpu
from jax.sharding import PartitionSpec as P

MEAN_REV = 0.05
STEP_YEARS = 0.25
HORIZON_YEARS = 30.0
SHARPNESS = 4.0
LOSS_RATE = 0.6
BASE = 128
LANES = 128
LARGE = 58 << 20
MIDDLE = 50 << 20
LOG2E = math.log2(math.e)
DECAY = math.exp(-MEAN_REV * STEP_YEARS)
HIGHEST = lax.Precision.HIGHEST
F32 = jnp.float32
BF16 = jnp.bfloat16


def round_up(size, step):
    return -(-size // step) * step


def exchange(copies, groups=None):
    return lax.all_to_all(copies, "path", 0, 0, axis_index_groups=groups)


def split(value, terms):
    parts = []
    for _ in range(terms):
        part = value.astype(BF16)
        parts.append(part)
        value = value - part.astype(F32)
    return parts


def contract(lhs, rhs, lhs_dim, rhs_dim, precision=None):
    return lax.dot_general(
        lhs,
        rhs,
        (((lhs_dim,), (rhs_dim,)), ((), ())),
        precision=precision,
        preferred_element_type=F32,
    )


def folded(parts, rows):
    total = parts[:rows]
    for first in range(rows, parts.shape[0], rows):
        total = total + parts[first : first + rows]
    return total


def stack(value):
    return jnp.concatenate(split(value, 3), axis=0)


def each(count, body, group=1):
    def step(index, carry):
        for offset in range(group):
            body(index * group + offset)
        return carry

    lax.fori_loop(0, count // group, step, 0)


def copy_of(source, target, sems, index):
    return pltpu.make_async_copy(source.at[index], target.at[index], sems.at[index])


def date_rows(date, knot_count):
    point = lax.broadcasted_iota(jnp.int32, (1, knot_count), 1) + 1
    alive = 120 * point > knot_count * (date + 1)
    maturity = HORIZON_YEARS * point.astype(F32) / knot_count
    fixing = STEP_YEARS * (date + 1).astype(F32)
    horizon = jnp.where(alive, maturity - fixing, 0.0)
    loading = (1.0 - jnp.exp(-MEAN_REV * horizon)) / MEAN_REV
    return alive, horizon, loading


def member_rows(flows, knot_count, set_count):
    digits = flows[:, knot_count : knot_count + 2].astype(F32)
    sets = (digits[:, 0:1] * BASE + digits[:, 1:2]).astype(jnp.int32)
    labels = lax.broadcasted_iota(jnp.int32, (flows.shape[0], set_count), 1)
    return sets == labels


def prep_kernel(end_ref, set_ref, cash_ref, out_ref):
    shards, trades, width = out_ref.shape
    knot_count = cash_ref.shape[1]
    row = lax.broadcasted_iota(jnp.int32, (trades, width), 0)
    point = lax.broadcasted_iota(jnp.int32, (trades, width), 1)
    ends = jnp.zeros((trades, width), jnp.int32)
    sets = jnp.zeros((trades, width), jnp.int32)
    for trade in range(trades):
        ends = jnp.where(row == trade, end_ref[trade], ends)
        sets = jnp.where(row == trade, set_ref[trade], sets)
    cash = jnp.concatenate(
        [cash_ref[...].astype(F32), jnp.zeros((trades, width - knot_count), F32)], axis=1
    )
    high = lax.shift_right_logical(sets, BASE.bit_length() - 1)
    low = sets & (BASE - 1)
    flows = jnp.where(point < jnp.minimum(ends, knot_count), cash, 0.0)
    flows = jnp.where(point == knot_count, high.astype(F32), flows)
    flows = jnp.where(point == knot_count + 1, low.astype(F32), flows).astype(BF16)
    for shard in range(shards):
        out_ref[shard] = flows


def feature_kernel(
    vol_hbm, normals_hbm, start_hbm, load_hbm, knots_hbm, jac_hbm,
    exact_hbm, feat_sum_ref,
    exact_buf, jac_buf, exact_sems, jac_sems, sems, normals_ref, state, load_ref, knots_ref, stacked, column, rate_ref, vol_ref,
):
    dates = normals_ref.shape[0]
    blocks, rows, knot_count = jac_hbm.shape
    inputs = [
        pltpu.make_async_copy(source, target, sems.at[place])
        for place, (source, target) in enumerate(
            ((load_hbm, load_ref), (knots_hbm, knots_ref), (start_hbm, state), (normals_hbm, normals_ref), (vol_hbm, vol_ref))
        )
    ]
    for copy in inputs:
        copy.start()
    each(blocks, lambda block: copy_of(jac_hbm, jac_buf, jac_sems, block).start())
    inputs[0].wait()
    high, middle, low = split(load_ref[...], 3)
    stacked[...] = jnp.concatenate([high, middle, high, middle, low, high], axis=0)
    for copy in inputs[1:]:
        copy.wait()

    parts = exact_sems.shape[0] // dates
    size = exact_buf.shape[1] // parts

    def sent(date, part):
        cut = pl.ds(part * size, size)
        sem = exact_sems.at[date * parts + part]
        return pltpu.make_async_copy(exact_buf.at[date, cut], exact_hbm.at[date, cut], sem)

    def zero_rates(block):
        copy_of(jac_hbm, jac_buf, jac_sems, block).wait()
        sums = jnp.sum(jac_buf[block] * knots_ref[...], axis=1, keepdims=True)
        column[pl.ds(pl.multiple_of(block * rows, rows), rows), :] = jnp.broadcast_to(sums, (rows, LANES))

    each(blocks, zero_rates)
    rate_ref[...] = column[...].T[0:1]

    def one(date):
        now = DECAY * state[...] + vol_ref[date] * normals_ref[date]
        state[...] = now
        high, middle, low = split(now, 3)
        terms = jnp.concatenate([high, high, middle, middle, high, low], axis=0)
        alive, horizon, loading = date_rows(date, knot_count)
        discount = jnp.where(alive, jnp.exp(-rate_ref[...] * horizon), 0.0)
        shift = contract(terms, stacked[...], 0, 0)
        exact = discount * jnp.exp2((-LOG2E * loading) * shift)
        exact_buf[date] = exact
        for part in range(parts):
            sent(date, part).start()
        row = pl.ds(date, 1)
        ones = jnp.ones((8, exact.shape[0]), BF16)
        feat_sum_ref[row, :] = contract(ones, exact.astype(BF16), 1, 0)[0:1]

    each(dates, one, dates)
    for part in range(parts):
        each(dates, lambda date, part=part: sent(date, part).wait())


def half_kernel(own_ref, feat_sum_ref, half_ref, terms_ref):
    knot_count, sets = half_ref.shape
    flows = own_ref[...]
    member = member_rows(flows, knot_count, sets).astype(BF16)
    half_ref[...] = contract(flows[:, :knot_count], member, 0, 0)
    terms_ref[...] = stack(feat_sum_ref[...])


def net_kernel(own_ref, other_ref, half_ref, terms_ref, flows_ref, net_ref, out_ref):
    knot_count, sets = net_ref.shape
    flows_ref[...] = jnp.concatenate([own_ref[...], other_ref[...]], axis=0)
    flows = other_ref[...]
    member = member_rows(flows, knot_count, sets).astype(BF16)
    net = (half_ref[...] + contract(flows[:, :knot_count], member, 0, 0)).astype(BF16)
    net_ref[...] = net
    sums = folded(contract(terms_ref[...], net, 1, 0), out_ref.shape[1])
    out_ref[...] = jnp.broadcast_to(sums[None], out_ref.shape)


def value_kernel(
    flows_ref, net_ref, cpty_ref, prob_ref, exact_hbm, values_ref, rows_ref, weight_ref, exact_buf, sems
):
    dates = values_ref.shape[0]
    each(dates, lambda date: copy_of(exact_hbm, exact_buf, sems, date).start())
    labels = lax.broadcasted_iota(jnp.int32, (prob_ref.shape[1], cpty_ref.shape[1]), 0)
    chosen = (cpty_ref[...] == labels).astype(F32)
    weight_ref[...] = LOSS_RATE * contract(prob_ref[...], chosen, 1, 0, HIGHEST)
    sets, knot_count = rows_ref.shape
    half = flows_ref.shape[0] // 2
    rows = []
    for first in (0, half):
        flows = flows_ref[first : first + half, :]
        member = member_rows(flows, knot_count, sets).astype(BF16)
        rows.append(contract(member, flows[:, :knot_count], 0, 0))
    rows_ref[...] = (rows[0] + rows[1]).astype(BF16)

    def one(date):
        copy_of(exact_hbm, exact_buf, sems, date).wait()
        values_ref[date] = contract(exact_buf[date].astype(BF16), net_ref[...], 1, 0)

    each(dates, one)


def slope_of(values, mean, base, weight):
    return weight * jax.nn.sigmoid(SHARPNESS * (values - mean + base))


def slope_kernel(paths, arrived_ref, values_ref, weight_ref, base_ref, mean_ref, sums_ref, out_ref):
    mean_ref[...] = jnp.sum(arrived_ref[...], axis=0) / paths
    for date in range(values_ref.shape[0]):
        row = slice(date, date + 1)
        slope = slope_of(values_ref[date], mean_ref[row, :], base_ref[row, :], weight_ref[row, :])
        sums_ref[row, :] = jnp.sum(slope, axis=0, keepdims=True)
    out_ref[...] = jnp.broadcast_to(sums_ref[...][None], out_ref.shape)


def adjoint_kernel(
    mean_ref, sums_ref, weight_ref, base_ref, feat_sum_ref, values_ref, net_ref, flows_ref, exact_hbm,
    blend_ref, rate_ref, trades_ref, cross_ref, exact_buf, sems, rate, loads,
):
    dates = values_ref.shape[0]
    paths, knot_count = blend_ref.shape
    each(dates, lambda date: copy_of(exact_hbm, exact_buf, sems, date).start())
    blend_ref[...] = jnp.zeros_like(blend_ref)
    rate[...] = jnp.zeros_like(rate)
    loads[...] = jnp.zeros_like(loads)
    flows = flows_ref[...]
    member = member_rows(flows, knot_count, net_ref.shape[0])
    flows = flows[:, :knot_count]
    cross_ref[...] = folded(contract(stack(feat_sum_ref[...]), flows, 1, 1), dates)

    def one(date):
        _, horizon, loading = date_rows(date, knot_count)
        factor = loading * jnp.exp(-MEAN_REV * STEP_YEARS * (date + 1).astype(F32))
        row = pl.ds(date, 1)
        slope = slope_of(values_ref[date], mean_ref[row, :], base_ref[row, :], weight_ref[row, :])
        adjoint = (slope - sums_ref[row, :] / paths).astype(BF16)
        copy_of(exact_hbm, exact_buf, sems, date).wait()
        exact = exact_buf[date]
        product = contract(adjoint, net_ref[...], 1, 0) * exact
        blend_ref[...] += factor * product
        rate[...] += horizon * jnp.sum(product.reshape(-1, 8, knot_count), axis=0)
        loads[...] += contract(adjoint, exact.astype(BF16), 0, 0)

    each(dates, one, 2 - dates % 2)
    shares = jnp.zeros(member.shape, F32)
    for part in split(loads[...], 3):
        shares = shares + contract(flows, part, 1, 1)
    trades_ref[...] = jnp.sum(jnp.where(member, shares, 0.0).T, axis=0, keepdims=True)
    rate_ref[...] = jnp.sum(rate[...], axis=0, keepdims=True)


def finish_kernel(
    paths, local, parity_ref, arrived_ref, sums_ref, feat_sum_ref, net_ref, flows_ref, rate_ref, trades_ref, cross_ref,
    shift_ref, out_ref,
):
    sets, knot_count = net_ref.shape
    gap = sums_ref[...] / local - jnp.sum(arrived_ref[...], axis=0) / paths
    flows = flows_ref[...]
    member = member_rows(flows, knot_count, sets).astype(BF16)
    terms = stack(gap)
    spread = folded(contract(terms, member, 1, 1), gap.shape[0])
    adjoint = folded(contract(terms, net_ref[...], 1, 0), gap.shape[0])
    total = rate_ref[...]
    for date in range(shift_ref.shape[0]):
        row = slice(date, date + 1)
        _, horizon, loading = date_rows(jnp.int32(date), knot_count)
        shift_ref[row, :] = loading * math.exp(-MEAN_REV * STEP_YEARS * (date + 1)) * adjoint[row]
        total = total + horizon * adjoint[row] * feat_sum_ref[row, :]
    trades = trades_ref[...] + jnp.sum(spread * cross_ref[...], axis=0, keepdims=True)
    count = trades.shape[1]
    trades = pltpu.roll(jnp.broadcast_to(trades, (8, count)), parity_ref[0] * (count // 2), 1)[0:1]
    shards, _, width = out_ref.shape
    pad = jnp.zeros((1, width - knot_count - trades.shape[1]), F32)
    row = jnp.concatenate([-total / paths, pad, trades / paths], axis=1)
    out_ref[...] = jnp.broadcast_to(row[None], out_ref.shape)


def start_kernel(
    blend_ref, shift_ref, load_ref, later_ref, exact_hbm, jac_hbm, out_ref, kept_ref, exact_buf, sems, jac_sems, blend
):
    dates = shift_ref.shape[0]
    kept = kept_ref.shape[0]
    each(dates, lambda date: copy_of(exact_hbm, exact_buf, sems, date).start())
    each(kept, lambda block: copy_of(jac_hbm, kept_ref, jac_sems, block).start())
    blend[...] = blend_ref[...]

    def one(date):
        copy_of(exact_hbm, exact_buf, sems, date).wait()
        blend[...] += shift_ref[pl.ds(date, 1), :] * exact_buf[date]

    each(dates, one)
    carried = contract(load_ref[...], blend[...], 1, 1, HIGHEST)
    out_ref[...] = math.exp(-MEAN_REV * STEP_YEARS * dates) * later_ref[...] - carried
    each(kept, lambda block: copy_of(jac_hbm, kept_ref, jac_sems, block).wait())


def final_kernel(index_ref, arrived_ref, kept_ref, jac_hbm, knot_ref, alloc_ref, jac_buf, sems, column, total):
    blocks, rows, knot_count = jac_hbm.shape
    kept = kept_ref.shape[0]
    missing = blocks - kept

    def fetched(block):
        return pltpu.make_async_copy(jac_hbm.at[kept + block], jac_buf.at[block], sems.at[block])

    each(missing, lambda block: fetched(block).start())
    row = jnp.sum(arrived_ref[...], axis=0)
    trades = alloc_ref.shape[1]
    parts = row[:, round_up(knot_count, LANES) :]
    count = parts.shape[1]
    offset = index_ref[0]
    parts = jnp.broadcast_to(parts, (8, count))
    alloc_ref[...] = pltpu.roll(parts, lax.rem(count - offset, count), 1)[0:1, :trades]
    column[...] = jnp.broadcast_to(row[:, :knot_count], (LANES, knot_count)).T
    total[...] = jnp.zeros_like(total)

    def add(source, block, first_block):
        part = column[pl.ds(pl.multiple_of((first_block + block) * rows, rows), rows), :]
        for first in range(0, knot_count, LANES):
            size = min(LANES, knot_count - first)
            cut = slice(first, first + size)
            scaled = source[block, :, cut] * part[:, :size]
            total[:, cut] += jnp.sum(scaled.reshape(-1, total.shape[0], size), axis=0)

    def late(block):
        fetched(block).wait()
        add(jac_buf, block, kept)

    each(kept, lambda block: add(kept_ref, block, 0))
    each(missing, late)
    knot_ref[...] = jnp.sum(total[...], axis=0, keepdims=True)


VMEM = pl.BlockSpec(memory_space=pltpu.VMEM)
SMEM = pl.BlockSpec(memory_space=pltpu.SMEM)


def shaped(shape, dtype=F32):
    return jax.ShapeDtypeStruct(shape, dtype)


def held(array):
    size = array.dtype.itemsize
    rows = array.shape[-2] if len(array.shape) > 1 else 1
    lead = math.prod(array.shape[:-2])
    return lead * round_up(rows, 8) * round_up(array.shape[-1], LANES) * size


def run(name, kernel, out_shape, operands, scalars=0, hbm=(), scratch=(), copies=(), buffers=1, smem=(), flops=0, grant=0):
    arrays = list(operands) + list(out_shape)
    room = sum(held(array) for array in scratch) + (8 << 20)
    specs = []
    for place, array in enumerate(arrays):
        if place < scalars:
            specs.append(SMEM)
        elif place in hbm:
            specs.append(pl.BlockSpec(memory_space=pltpu.HBM))
        else:
            specs.append(VMEM)
            room += held(array)
    moved = sum(held(array) for array in arrays)
    return pl.pallas_call(
        kernel,
        out_shape=tuple(out_shape),
        in_specs=specs[: len(operands)],
        out_specs=tuple(specs[len(operands) :]),
        scratch_shapes=[pltpu.VMEM(array.shape, array.dtype) for array in scratch[:buffers]]
        + [pltpu.SemaphoreType.DMA((count,)) for count in copies]
        + [pltpu.VMEM(array.shape, array.dtype) for array in scratch[buffers:]]
        + [pltpu.SMEM(array.shape, array.dtype) for array in smem],
        compiler_params=pltpu.CompilerParams(vmem_limit_bytes=grant or room),
        cost_estimate=pl.CostEstimate(flops=flops, bytes_accessed=moved, transcendentals=0),
        name=name,
    )(*operands)


def per_device(
    normals,
    start_state,
    later_adjoint,
    vol,
    factor_load,
    knots,
    spline_jac,
    cashflows,
    trade_set,
    trade_end,
    set_cpty,
    default_prob,
    base_value,
):
    dates, factors, paths = normals.shape
    knot_count = knots.shape[0]
    sets = base_value.shape[1]
    shards = lax.axis_size("path")
    trades = cashflows.shape[0]
    all_trades = trades * shards
    all_paths = paths * shards
    width = round_up(knot_count + 2, LANES)
    work = 2 * dates * paths * knot_count
    grid_rows = shaped((dates, knot_count))
    set_rows = shaped((dates, sets))
    set_copies = shaped((shards, dates, sets))

    (copies,) = run(
        "prep",
        prep_kernel,
        [shaped((shards // 2, trades, width), BF16)],
        [trade_end, trade_set.reshape(trades), cashflows],
        scalars=2,
        grant=LARGE,
    )
    own = exchange(copies, [list(range(side, shards, 2)) for side in range(2)])
    own = own.reshape(all_trades // 2, width)
    index = lax.axis_index("path").astype(jnp.int32)
    parity = lax.rem(index, 2)
    offset = parity * (all_trades // 2) + lax.div(index, 2) * trades
    blocks = next(count for count in (8, 4, 2, 1) if knot_count % (8 * count) == 0)
    jac_blocks = spline_jac.reshape(blocks, knot_count // blocks, knot_count)

    exact, feat_sums = run(
        "features",
        feature_kernel,
        [shaped((dates, paths, knot_count)), grid_rows],
        [vol, normals, start_state, factor_load, knots.reshape(1, knot_count), jac_blocks],
        hbm=(0, 1, 2, 3, 4, 5, 6),
        scratch=[
            shaped((dates, paths, knot_count)),
            shaped(jac_blocks.shape),
            shaped(normals.shape),
            shaped(start_state.shape),
            shaped(factor_load.shape),
            shaped((1, knot_count)),
            shaped((6 * factors, knot_count), BF16),
            shaped((knot_count, LANES)),
            shaped((1, knot_count)),
        ],
        buffers=2,
        copies=(dates * (4 if paths % 64 == 0 else 1), blocks, 5),
        smem=(shaped(vol.shape),),
        flops=6 * factors * work,
        grant=LARGE,
    )

    own, feat_sums = lax.optimization_barrier((own, feat_sums))
    other = lax.ppermute(own, "path", [(shard, shard ^ 1) for shard in range(shards)])
    half, terms = run(
        "half",
        half_kernel,
        [shaped((knot_count, sets)), shaped((3 * dates, knot_count), BF16)],
        [own, feat_sums],
        flops=sets * all_trades * knot_count,
    )
    flows, net_columns, copies = run(
        "net",
        net_kernel,
        [shaped((all_trades, width), BF16), shaped((knot_count, sets), BF16), set_copies],
        [own, other, half, terms],
        flops=sets * all_trades * knot_count,
    )
    arrived = exchange(copies)
    values, net_rows, weight = run(
        "values",
        value_kernel,
        [shaped((dates, paths, sets)), shaped((sets, knot_count), BF16), set_rows],
        [flows, net_columns, set_cpty.reshape(1, sets), default_prob, exact],
        hbm=(4,),
        scratch=[shaped((dates, paths, knot_count))],
        copies=(dates,),
        flops=sets * work,
        grant=MIDDLE,
    )
    mean, slope_sums, copies = run(
        "slopes",
        functools.partial(slope_kernel, all_paths),
        [set_rows, set_rows, set_copies],
        [arrived, values, weight, base_value],
        flops=16 * dates * paths * sets,
    )
    arrived = exchange(copies)
    blend, rate, trade_parts, cross = run(
        "adjoint",
        adjoint_kernel,
        [
            shaped((paths, knot_count)),
            shaped((1, knot_count)),
            shaped((1, all_trades)),
            shaped((dates, all_trades)),
        ],
        [mean, slope_sums, weight, base_value, feat_sums, values, net_rows, flows, exact],
        hbm=(8,),
        scratch=[
            shaped((dates, paths, knot_count)),
            shaped((8, knot_count)),
            shaped((sets, knot_count)),
        ],
        copies=(dates,),
        flops=2 * sets * work,
        grant=MIDDLE,
    )
    row_width = round_up(knot_count, LANES) + all_trades
    shift, copies = run(
        "finish",
        functools.partial(finish_kernel, all_paths, paths),
        [grid_rows, shaped((shards, 1, row_width))],
        [parity.reshape(1), arrived, slope_sums, feat_sums, net_rows, flows, rate, trade_parts, cross],
        scalars=1,
        flops=6 * sets * dates * knot_count,
    )
    arrived = exchange(copies)
    kept = blocks * 4 // 8
    start_adjoint, kept_blocks = run(
        "start",
        start_kernel,
        [shaped((factors, paths)), shaped((kept,) + jac_blocks.shape[1:])],
        [blend, shift, factor_load, later_adjoint, exact, jac_blocks],
        hbm=(4, 5),
        scratch=[shaped((dates, paths, knot_count)), shaped((paths, knot_count))],
        copies=(dates, kept),
        flops=2 * factors * paths * knot_count,
        grant=49<<20,
    )
    knot_grad, alloc = run(
        "final",
        final_kernel,
        [shaped((1, knot_count)), shaped((1, trades))],
        [offset.reshape(1), arrived, kept_blocks, jac_blocks],
        scalars=1,
        hbm=(3,),
        scratch=[
            shaped((blocks - kept,) + jac_blocks.shape[1:]),
            shaped((knot_count, LANES)),
            shaped((8, knot_count)),
        ],
        copies=(blocks - kept,),
        flops=2 * knot_count**2,
        grant=51<<20,
    )
    return knot_grad.reshape(knot_count), alloc.reshape(trades), start_adjoint


def solution(mesh):
    in_specs = (
        P(None, None, ("group", "path")),
        P(None, ("group", "path")),
        P(None, ("group", "path")),
        P(),
        P(),
        P(),
        P(),
        P(("group", "path"), None),
        P(("group", "path"), None),
        P(("group", "path")),
        P("group", None),
        P(),
        P(None, "group"),
    )
    out_specs = (P("group"), P(("group", "path")), P(None, ("group", "path")))
    return jax.shard_map(
        per_device, mesh=mesh, in_specs=in_specs, out_specs=out_specs, check_vma=False
    )
```

```python
import functools
import math

import jax
import jax.numpy as jnp
from jax import lax
from jax.experimental import pallas as pl
from jax.experimental.pallas import tpu as pltpu
from jax.sharding import PartitionSpec as P

MEAN_REV = 0.05
STEP_YEARS = 0.25
HORIZON_YEARS = 30.0
SHARPNESS = 4.0
LOSS_RATE = 0.6
BASE = 128
LANES = 128
LARGE = 58 << 20
MIDDLE = 50 << 20
LOG2E = math.log2(math.e)
DECAY = math.exp(-MEAN_REV * STEP_YEARS)
HIGHEST = lax.Precision.HIGHEST
F32 = jnp.float32
BF16 = jnp.bfloat16


def round_up(size, step):
    return -(-size // step) * step


def exchange(copies, groups=None):
    return lax.all_to_all(copies, "path", 0, 0, axis_index_groups=groups)


def split(value, terms):
    parts = []
    for _ in range(terms):
        part = value.astype(BF16)
        parts.append(part)
        value = value - part.astype(F32)
    return parts


def contract(lhs, rhs, lhs_dim, rhs_dim, precision=None):
    return lax.dot_general(
        lhs,
        rhs,
        (((lhs_dim,), (rhs_dim,)), ((), ())),
        precision=precision,
        preferred_element_type=F32,
    )


def folded(parts, rows):
    total = parts[:rows]
    for first in range(rows, parts.shape[0], rows):
        total = total + parts[first : first + rows]
    return total


def stack(value):
    return jnp.concatenate(split(value, 3), axis=0)


def each(count, body, group=1):
    def step(index, carry):
        for offset in range(group):
            body(index * group + offset)
        return carry

    lax.fori_loop(0, count // group, step, 0)


def copy_of(source, target, sems, index):
    return pltpu.make_async_copy(source.at[index], target.at[index], sems.at[index])


def date_rows(date, knot_count):
    point = lax.broadcasted_iota(jnp.int32, (1, knot_count), 1) + 1
    alive = 120 * point > knot_count * (date + 1)
    maturity = HORIZON_YEARS * point.astype(F32) / knot_count
    fixing = STEP_YEARS * (date + 1).astype(F32)
    horizon = jnp.where(alive, maturity - fixing, 0.0)
    loading = (1.0 - jnp.exp(-MEAN_REV * horizon)) / MEAN_REV
    return alive, horizon, loading


def member_rows(flows, knot_count, set_count):
    digits = flows[:, knot_count : knot_count + 2].astype(F32)
    sets = (digits[:, 0:1] * BASE + digits[:, 1:2]).astype(jnp.int32)
    labels = lax.broadcasted_iota(jnp.int32, (flows.shape[0], set_count), 1)
    return sets == labels


def prep_kernel(end_ref, set_ref, cash_ref, out_ref):
    shards, trades, width = out_ref.shape
    knot_count = cash_ref.shape[1]
    row = lax.broadcasted_iota(jnp.int32, (trades, width), 0)
    point = lax.broadcasted_iota(jnp.int32, (trades, width), 1)
    ends = jnp.zeros((trades, width), jnp.int32)
    sets = jnp.zeros((trades, width), jnp.int32)
    for trade in range(trades):
        ends = jnp.where(row == trade, end_ref[trade], ends)
        sets = jnp.where(row == trade, set_ref[trade], sets)
    cash = jnp.concatenate(
        [cash_ref[...].astype(F32), jnp.zeros((trades, width - knot_count), F32)], axis=1
    )
    high = lax.shift_right_logical(sets, BASE.bit_length() - 1)
    low = sets & (BASE - 1)
    flows = jnp.where(point < jnp.minimum(ends, knot_count), cash, 0.0)
    flows = jnp.where(point == knot_count, high.astype(F32), flows)
    flows = jnp.where(point == knot_count + 1, low.astype(F32), flows).astype(BF16)
    for shard in range(shards):
        out_ref[shard] = flows


def feature_kernel(
    vol_hbm, normals_hbm, start_hbm, load_hbm, knots_hbm, jac_hbm,
    exact_hbm, feat_sum_ref,
    exact_buf, jac_buf, exact_sems, jac_sems, sems, normals_ref, state, load_ref, knots_ref, stacked, column, rate_ref, vol_ref,
):
    dates = normals_ref.shape[0]
    blocks, rows, knot_count = jac_hbm.shape
    inputs = [
        pltpu.make_async_copy(source, target, sems.at[place])
        for place, (source, target) in enumerate(
            ((load_hbm, load_ref), (knots_hbm, knots_ref), (start_hbm, state), (normals_hbm, normals_ref), (vol_hbm, vol_ref))
        )
    ]
    for copy in inputs:
        copy.start()
    each(blocks, lambda block: copy_of(jac_hbm, jac_buf, jac_sems, block).start())
    inputs[0].wait()
    high, middle, low = split(load_ref[...], 3)
    stacked[...] = jnp.concatenate([high, middle, high, middle, low, high], axis=0)
    for copy in inputs[1:]:
        copy.wait()

    parts = exact_sems.shape[0] // dates
    size = exact_buf.shape[1] // parts

    def sent(date, part):
        cut = pl.ds(part * size, size)
        sem = exact_sems.at[date * parts + part]
        return pltpu.make_async_copy(exact_buf.at[date, cut], exact_hbm.at[date, cut], sem)

    def zero_rates(block):
        copy_of(jac_hbm, jac_buf, jac_sems, block).wait()
        sums = jnp.sum(jac_buf[block] * knots_ref[...], axis=1, keepdims=True)
        column[pl.ds(pl.multiple_of(block * rows, rows), rows), :] = jnp.broadcast_to(sums, (rows, LANES))

    each(blocks, zero_rates)
    rate_ref[...] = column[...].T[0:1]

    def one(date):
        now = DECAY * state[...] + vol_ref[date] * normals_ref[date]
        state[...] = now
        high, middle, low = split(now, 3)
        terms = jnp.concatenate([high, high, middle, middle, high, low], axis=0)
        alive, horizon, loading = date_rows(date, knot_count)
        discount = jnp.where(alive, jnp.exp(-rate_ref[...] * horizon), 0.0)
        shift = contract(terms, stacked[...], 0, 0)
        exact = discount * jnp.exp2((-LOG2E * loading) * shift)
        exact_buf[date] = exact
        for part in range(parts):
            sent(date, part).start()
        row = pl.ds(date, 1)
        ones = jnp.ones((8, exact.shape[0]), BF16)
        feat_sum_ref[row, :] = contract(ones, exact.astype(BF16), 1, 0)[0:1]

    each(dates, one, dates)
    for part in range(parts):
        each(dates, lambda date, part=part: sent(date, part).wait())


def half_kernel(own_ref, feat_sum_ref, half_ref, terms_ref):
    knot_count, sets = half_ref.shape
    flows = own_ref[...]
    member = member_rows(flows, knot_count, sets).astype(BF16)
    half_ref[...] = contract(flows[:, :knot_count], member, 0, 0)
    terms_ref[...] = stack(feat_sum_ref[...])


def net_kernel(own_ref, other_ref, half_ref, terms_ref, flows_ref, net_ref, out_ref):
    knot_count, sets = net_ref.shape
    flows_ref[...] = jnp.concatenate([own_ref[...], other_ref[...]], axis=0)
    flows = other_ref[...]
    member = member_rows(flows, knot_count, sets).astype(BF16)
    net = (half_ref[...] + contract(flows[:, :knot_count], member, 0, 0)).astype(BF16)
    net_ref[...] = net
    sums = folded(contract(terms_ref[...], net, 1, 0), out_ref.shape[1])
    out_ref[...] = jnp.broadcast_to(sums[None], out_ref.shape)


def value_kernel(
    flows_ref, net_ref, cpty_ref, prob_ref, exact_hbm, values_ref, rows_ref, weight_ref, exact_buf, sems
):
    dates = values_ref.shape[0]
    each(dates, lambda date: copy_of(exact_hbm, exact_buf, sems, date).start())
    labels = lax.broadcasted_iota(jnp.int32, (prob_ref.shape[1], cpty_ref.shape[1]), 0)
    chosen = (cpty_ref[...] == labels).astype(F32)
    weight_ref[...] = LOSS_RATE * contract(prob_ref[...], chosen, 1, 0, HIGHEST)
    sets, knot_count = rows_ref.shape
    half = flows_ref.shape[0] // 2
    rows = []
    for first in (0, half):
        flows = flows_ref[first : first + half, :]
        member = member_rows(flows, knot_count, sets).astype(BF16)
        rows.append(contract(member, flows[:, :knot_count], 0, 0))
    rows_ref[...] = (rows[0] + rows[1]).astype(BF16)

    def one(date):
        copy_of(exact_hbm, exact_buf, sems, date).wait()
        values_ref[date] = contract(exact_buf[date].astype(BF16), net_ref[...], 1, 0)

    each(dates, one)


def slope_of(values, mean, base, weight):
    return weight * jax.nn.sigmoid(SHARPNESS * (values - mean + base))


def slope_kernel(paths, arrived_ref, values_ref, weight_ref, base_ref, mean_ref, sums_ref, out_ref):
    mean_ref[...] = jnp.sum(arrived_ref[...], axis=0) / paths
    for date in range(values_ref.shape[0]):
        row = slice(date, date + 1)
        slope = slope_of(values_ref[date], mean_ref[row, :], base_ref[row, :], weight_ref[row, :])
        sums_ref[row, :] = jnp.sum(slope, axis=0, keepdims=True)
    out_ref[...] = jnp.broadcast_to(sums_ref[...][None], out_ref.shape)


def adjoint_kernel(
    mean_ref, sums_ref, weight_ref, base_ref, feat_sum_ref, values_ref, net_ref, flows_ref, exact_hbm,
    blend_ref, rate_ref, trades_ref, cross_ref, exact_buf, sems, rate, loads,
):
    dates = values_ref.shape[0]
    paths, knot_count = blend_ref.shape
    each(dates, lambda date: copy_of(exact_hbm, exact_buf, sems, date).start())
    blend_ref[...] = jnp.zeros_like(blend_ref)
    rate[...] = jnp.zeros_like(rate)
    loads[...] = jnp.zeros_like(loads)
    flows = flows_ref[...]
    member = member_rows(flows, knot_count, net_ref.shape[0])
    flows = flows[:, :knot_count]
    cross_ref[...] = folded(contract(stack(feat_sum_ref[...]), flows, 1, 1), dates)

    def one(date):
        _, horizon, loading = date_rows(date, knot_count)
        factor = loading * jnp.exp(-MEAN_REV * STEP_YEARS * (date + 1).astype(F32))
        row = pl.ds(date, 1)
        slope = slope_of(values_ref[date], mean_ref[row, :], base_ref[row, :], weight_ref[row, :])
        adjoint = (slope - sums_ref[row, :] / paths).astype(BF16)
        copy_of(exact_hbm, exact_buf, sems, date).wait()
        exact = exact_buf[date]
        product = contract(adjoint, net_ref[...], 1, 0) * exact
        blend_ref[...] += factor * product
        rate[...] += horizon * jnp.sum(product.reshape(-1, 8, knot_count), axis=0)
        loads[...] += contract(adjoint, exact.astype(BF16), 0, 0)

    each(dates, one, 2 - dates % 2)
    shares = jnp.zeros(member.shape, F32)
    for part in split(loads[...], 3):
        shares = shares + contract(flows, part, 1, 1)
    trades_ref[...] = jnp.sum(jnp.where(member, shares, 0.0).T, axis=0, keepdims=True)
    rate_ref[...] = jnp.sum(rate[...], axis=0, keepdims=True)


def finish_kernel(
    paths, local, parity_ref, arrived_ref, sums_ref, feat_sum_ref, net_ref, flows_ref, rate_ref, trades_ref, cross_ref,
    shift_ref, out_ref,
):
    sets, knot_count = net_ref.shape
    gap = sums_ref[...] / local - jnp.sum(arrived_ref[...], axis=0) / paths
    flows = flows_ref[...]
    member = member_rows(flows, knot_count, sets).astype(BF16)
    terms = stack(gap)
    spread = folded(contract(terms, member, 1, 1), gap.shape[0])
    adjoint = folded(contract(terms, net_ref[...], 1, 0), gap.shape[0])
    total = rate_ref[...]
    for date in range(shift_ref.shape[0]):
        row = slice(date, date + 1)
        _, horizon, loading = date_rows(jnp.int32(date), knot_count)
        shift_ref[row, :] = loading * math.exp(-MEAN_REV * STEP_YEARS * (date + 1)) * adjoint[row]
        total = total + horizon * adjoint[row] * feat_sum_ref[row, :]
    trades = trades_ref[...] + jnp.sum(spread * cross_ref[...], axis=0, keepdims=True)
    count = trades.shape[1]
    trades = pltpu.roll(jnp.broadcast_to(trades, (8, count)), parity_ref[0] * (count // 2), 1)[0:1]
    shards, _, width = out_ref.shape
    pad = jnp.zeros((1, width - knot_count - trades.shape[1]), F32)
    row = jnp.concatenate([-total / paths, pad, trades / paths], axis=1)
    out_ref[...] = jnp.broadcast_to(row[None], out_ref.shape)


def start_kernel(
    blend_ref, shift_ref, load_ref, later_ref, exact_hbm, jac_hbm, out_ref, kept_ref, exact_buf, sems, jac_sems, blend
):
    dates = shift_ref.shape[0]
    kept = kept_ref.shape[0]
    each(dates, lambda date: copy_of(exact_hbm, exact_buf, sems, date).start())
    each(kept, lambda block: copy_of(jac_hbm, kept_ref, jac_sems, block).start())
    blend[...] = blend_ref[...]

    def one(date):
        copy_of(exact_hbm, exact_buf, sems, date).wait()
        blend[...] += shift_ref[pl.ds(date, 1), :] * exact_buf[date]

    each(dates, one)
    carried = contract(load_ref[...], blend[...], 1, 1, HIGHEST)
    out_ref[...] = math.exp(-MEAN_REV * STEP_YEARS * dates) * later_ref[...] - carried
    each(kept, lambda block: copy_of(jac_hbm, kept_ref, jac_sems, block).wait())


def final_kernel(index_ref, arrived_ref, kept_ref, jac_hbm, knot_ref, alloc_ref, jac_buf, sems, column, total):
    blocks, rows, knot_count = jac_hbm.shape
    kept = kept_ref.shape[0]
    missing = blocks - kept

    def fetched(block):
        return pltpu.make_async_copy(jac_hbm.at[kept + block], jac_buf.at[block], sems.at[block])

    each(missing, lambda block: fetched(block).start())
    row = jnp.sum(arrived_ref[...], axis=0)
    trades = alloc_ref.shape[1]
    parts = row[:, round_up(knot_count, LANES) :]
    count = parts.shape[1]
    offset = index_ref[0]
    parts = jnp.broadcast_to(parts, (8, count))
    alloc_ref[...] = pltpu.roll(parts, lax.rem(count - offset, count), 1)[0:1, :trades]
    column[...] = jnp.broadcast_to(row[:, :knot_count], (LANES, knot_count)).T
    total[...] = jnp.zeros_like(total)

    def add(source, block, first_block):
        part = column[pl.ds(pl.multiple_of((first_block + block) * rows, rows), rows), :]
        for first in range(0, knot_count, LANES):
            size = min(LANES, knot_count - first)
            cut = slice(first, first + size)
            scaled = source[block, :, cut] * part[:, :size]
            total[:, cut] += jnp.sum(scaled.reshape(-1, total.shape[0], size), axis=0)

    def late(block):
        fetched(block).wait()
        add(jac_buf, block, kept)

    each(kept, lambda block: add(kept_ref, block, 0))
    each(missing, late)
    knot_ref[...] = jnp.sum(total[...], axis=0, keepdims=True)


VMEM = pl.BlockSpec(memory_space=pltpu.VMEM)
SMEM = pl.BlockSpec(memory_space=pltpu.SMEM)


def shaped(shape, dtype=F32):
    return jax.ShapeDtypeStruct(shape, dtype)


def held(array):
    size = array.dtype.itemsize
    rows = array.shape[-2] if len(array.shape) > 1 else 1
    lead = math.prod(array.shape[:-2])
    return lead * round_up(rows, 8) * round_up(array.shape[-1], LANES) * size


def run(name, kernel, out_shape, operands, scalars=0, hbm=(), scratch=(), copies=(), buffers=1, smem=(), flops=0, grant=0):
    arrays = list(operands) + list(out_shape)
    room = sum(held(array) for array in scratch) + (8 << 20)
    specs = []
    for place, array in enumerate(arrays):
        if place < scalars:
            specs.append(SMEM)
        elif place in hbm:
            specs.append(pl.BlockSpec(memory_space=pltpu.HBM))
        else:
            specs.append(VMEM)
            room += held(array)
    moved = sum(held(array) for array in arrays)
    return pl.pallas_call(
        kernel,
        out_shape=tuple(out_shape),
        in_specs=specs[: len(operands)],
        out_specs=tuple(specs[len(operands) :]),
        scratch_shapes=[pltpu.VMEM(array.shape, array.dtype) for array in scratch[:buffers]]
        + [pltpu.SemaphoreType.DMA((count,)) for count in copies]
        + [pltpu.VMEM(array.shape, array.dtype) for array in scratch[buffers:]]
        + [pltpu.SMEM(array.shape, array.dtype) for array in smem],
        compiler_params=pltpu.CompilerParams(vmem_limit_bytes=grant or room),
        cost_estimate=pl.CostEstimate(flops=flops, bytes_accessed=moved, transcendentals=0),
        name=name,
    )(*operands)


def per_device(
    normals,
    start_state,
    later_adjoint,
    vol,
    factor_load,
    knots,
    spline_jac,
    cashflows,
    trade_set,
    trade_end,
    set_cpty,
    default_prob,
    base_value,
):
    dates, factors, paths = normals.shape
    knot_count = knots.shape[0]
    sets = base_value.shape[1]
    shards = lax.axis_size("path")
    trades = cashflows.shape[0]
    all_trades = trades * shards
    all_paths = paths * shards
    width = round_up(knot_count + 2, LANES)
    work = 2 * dates * paths * knot_count
    grid_rows = shaped((dates, knot_count))
    set_rows = shaped((dates, sets))
    set_copies = shaped((shards, dates, sets))

    (copies,) = run(
        "prep",
        prep_kernel,
        [shaped((shards // 2, trades, width), BF16)],
        [trade_end, trade_set.reshape(trades), cashflows],
        scalars=2,
        grant=LARGE,
    )
    pairs = shards // 2
    places = [(2 * pairs - 1 - pair - pairs // 2) % pairs for pair in range(pairs)]
    own = exchange(copies, [[2 * pair + side for pair in places] for side in range(2)])
    own = own.reshape(all_trades // 2, width)
    index = lax.axis_index("path").astype(jnp.int32)
    parity = lax.rem(index, 2)
    place = lax.rem(2 * pairs - 1 - lax.div(index, 2) - pairs // 2, pairs)
    offset = parity * (all_trades // 2) + place * trades
    blocks = next(count for count in (8, 4, 2, 1) if knot_count % (8 * count) == 0)
    jac_blocks = spline_jac.reshape(blocks, knot_count // blocks, knot_count)

    exact, feat_sums = run(
        "features",
        feature_kernel,
        [shaped((dates, paths, knot_count)), grid_rows],
        [vol, normals, start_state, factor_load, knots.reshape(1, knot_count), jac_blocks],
        hbm=(0, 1, 2, 3, 4, 5, 6),
        scratch=[
            shaped((dates, paths, knot_count)),
            shaped(jac_blocks.shape),
            shaped(normals.shape),
            shaped(start_state.shape),
            shaped(factor_load.shape),
            shaped((1, knot_count)),
            shaped((6 * factors, knot_count), BF16),
            shaped((knot_count, LANES)),
            shaped((1, knot_count)),
        ],
        buffers=2,
        copies=(dates * (4 if paths % 64 == 0 else 1), blocks, 5),
        smem=(shaped(vol.shape),),
        flops=6 * factors * work,
        grant=LARGE,
    )

    own, feat_sums = lax.optimization_barrier((own, feat_sums))
    other = lax.ppermute(own, "path", [(shard, shard ^ 1) for shard in range(shards)])
    half, terms = run(
        "half",
        half_kernel,
        [shaped((knot_count, sets)), shaped((3 * dates, knot_count), BF16)],
        [own, feat_sums],
        flops=sets * all_trades * knot_count,
    )
    flows, net_columns, copies = run(
        "net",
        net_kernel,
        [shaped((all_trades, width), BF16), shaped((knot_count, sets), BF16), set_copies],
        [own, other, half, terms],
        flops=sets * all_trades * knot_count,
    )
    arrived = exchange(copies, [list(range(shards))[::-1]])
    values, net_rows, weight = run(
        "values",
        value_kernel,
        [shaped((dates, paths, sets)), shaped((sets, knot_count), BF16), set_rows],
        [flows, net_columns, set_cpty.reshape(1, sets), default_prob, exact],
        hbm=(4,),
        scratch=[shaped((dates, paths, knot_count))],
        copies=(dates,),
        flops=sets * work,
        grant=MIDDLE,
    )
    mean, slope_sums, copies = run(
        "slopes",
        functools.partial(slope_kernel, all_paths),
        [set_rows, set_rows, set_copies],
        [arrived, values, weight, base_value],
        flops=16 * dates * paths * sets,
    )
    arrived = exchange(copies, [list(range(shards))[::-1]])
    blend, rate, trade_parts, cross = run(
        "adjoint",
        adjoint_kernel,
        [
            shaped((paths, knot_count)),
            shaped((1, knot_count)),
            shaped((1, all_trades)),
            shaped((dates, all_trades)),
        ],
        [mean, slope_sums, weight, base_value, feat_sums, values, net_rows, flows, exact],
        hbm=(8,),
        scratch=[
            shaped((dates, paths, knot_count)),
            shaped((8, knot_count)),
            shaped((sets, knot_count)),
        ],
        copies=(dates,),
        flops=2 * sets * work,
        grant=MIDDLE,
    )
    row_width = round_up(knot_count, LANES) + all_trades
    shift, copies = run(
        "finish",
        functools.partial(finish_kernel, all_paths, paths),
        [grid_rows, shaped((shards, 1, row_width))],
        [parity.reshape(1), arrived, slope_sums, feat_sums, net_rows, flows, rate, trade_parts, cross],
        scalars=1,
        flops=6 * sets * dates * knot_count,
    )
    arrived = exchange(copies, [list(range(shards))[::-1]])
    kept = blocks * 4 // 8
    start_adjoint, kept_blocks = run(
        "start",
        start_kernel,
        [shaped((factors, paths)), shaped((kept,) + jac_blocks.shape[1:])],
        [blend, shift, factor_load, later_adjoint, exact, jac_blocks],
        hbm=(4, 5),
        scratch=[shaped((dates, paths, knot_count)), shaped((paths, knot_count))],
        copies=(dates, kept),
        flops=2 * factors * paths * knot_count,
        grant=49<<20,
    )
    knot_grad, alloc = run(
        "final",
        final_kernel,
        [shaped((1, knot_count)), shaped((1, trades))],
        [offset.reshape(1), arrived, kept_blocks, jac_blocks],
        scalars=1,
        hbm=(3,),
        scratch=[
            shaped((blocks - kept,) + jac_blocks.shape[1:]),
            shaped((knot_count, LANES)),
            shaped((8, knot_count)),
        ],
        copies=(blocks - kept,),
        flops=2 * knot_count**2,
        grant=51<<20,
    )
    return knot_grad.reshape(knot_count), alloc.reshape(trades), start_adjoint


def solution(mesh):
    in_specs = (
        P(None, None, ("group", "path")),
        P(None, ("group", "path")),
        P(None, ("group", "path")),
        P(),
        P(),
        P(),
        P(),
        P(("group", "path"), None),
        P(("group", "path"), None),
        P(("group", "path")),
        P("group", None),
        P(),
        P(None, "group"),
    )
    out_specs = (P("group"), P(("group", "path")), P(None, ("group", "path")))
    return jax.shard_map(
        per_device, mesh=mesh, in_specs=in_specs, out_specs=out_specs, check_vma=False
    )
```

```python
import functools
import math

import jax
import jax.numpy as jnp
from jax import lax
from jax.experimental import pallas as pl
from jax.experimental.pallas import tpu as pltpu
from jax.sharding import PartitionSpec as P

MEAN_REV = 0.05
STEP_YEARS = 0.25
HORIZON_YEARS = 30.0
SHARPNESS = 4.0
LOSS_RATE = 0.6
BASE = 128
LANES = 128
LARGE = 58 << 20
MIDDLE = 50 << 20
LOG2E = math.log2(math.e)
DECAY = math.exp(-MEAN_REV * STEP_YEARS)
HIGHEST = lax.Precision.HIGHEST
F32 = jnp.float32
BF16 = jnp.bfloat16


def round_up(size, step):
    return -(-size // step) * step


def exchange(copies, groups=None):
    return lax.all_to_all(copies, "path", 0, 0, axis_index_groups=groups)


def split(value, terms):
    parts = []
    for _ in range(terms):
        part = value.astype(BF16)
        parts.append(part)
        value = value - part.astype(F32)
    return parts


def contract(lhs, rhs, lhs_dim, rhs_dim, precision=None):
    return lax.dot_general(
        lhs,
        rhs,
        (((lhs_dim,), (rhs_dim,)), ((), ())),
        precision=precision,
        preferred_element_type=F32,
    )


def folded(parts, rows):
    total = parts[:rows]
    for first in range(rows, parts.shape[0], rows):
        total = total + parts[first : first + rows]
    return total


def stack(value):
    return jnp.concatenate(split(value, 3), axis=0)


def each(count, body, group=1):
    def step(index, carry):
        for offset in range(group):
            body(index * group + offset)
        return carry

    lax.fori_loop(0, count // group, step, 0)


def copy_of(source, target, sems, index):
    return pltpu.make_async_copy(source.at[index], target.at[index], sems.at[index])


def date_rows(date, knot_count):
    point = lax.broadcasted_iota(jnp.int32, (1, knot_count), 1) + 1
    alive = 120 * point > knot_count * (date + 1)
    maturity = HORIZON_YEARS * point.astype(F32) / knot_count
    fixing = STEP_YEARS * (date + 1).astype(F32)
    horizon = jnp.where(alive, maturity - fixing, 0.0)
    loading = (1.0 - jnp.exp(-MEAN_REV * horizon)) / MEAN_REV
    return alive, horizon, loading


def member_rows(flows, knot_count, set_count):
    digits = flows[:, knot_count : knot_count + 2].astype(F32)
    sets = (digits[:, 0:1] * BASE + digits[:, 1:2]).astype(jnp.int32)
    labels = lax.broadcasted_iota(jnp.int32, (flows.shape[0], set_count), 1)
    return sets == labels


def prep_kernel(end_ref, set_ref, cash_ref, out_ref):
    shards, trades, width = out_ref.shape
    knot_count = cash_ref.shape[1]
    row = lax.broadcasted_iota(jnp.int32, (trades, width), 0)
    point = lax.broadcasted_iota(jnp.int32, (trades, width), 1)
    ends = jnp.zeros((trades, width), jnp.int32)
    sets = jnp.zeros((trades, width), jnp.int32)
    for trade in range(trades):
        ends = jnp.where(row == trade, end_ref[trade], ends)
        sets = jnp.where(row == trade, set_ref[trade], sets)
    cash = jnp.concatenate(
        [cash_ref[...].astype(F32), jnp.zeros((trades, width - knot_count), F32)], axis=1
    )
    high = lax.shift_right_logical(sets, BASE.bit_length() - 1)
    low = sets & (BASE - 1)
    flows = jnp.where(point < jnp.minimum(ends, knot_count), cash, 0.0)
    flows = jnp.where(point == knot_count, high.astype(F32), flows)
    flows = jnp.where(point == knot_count + 1, low.astype(F32), flows).astype(BF16)
    for shard in range(shards):
        out_ref[shard] = flows


def feature_kernel(
    vol_hbm, normals_hbm, start_hbm, load_hbm, knots_hbm, jac_hbm,
    exact_hbm, feat_sum_ref,
    exact_buf, jac_buf, exact_sems, jac_sems, sems, normals_ref, state, load_ref, knots_ref, stacked, column, rate_ref, vol_ref,
):
    dates = normals_ref.shape[0]
    blocks, rows, knot_count = jac_hbm.shape
    inputs = [
        pltpu.make_async_copy(source, target, sems.at[place])
        for place, (source, target) in enumerate(
            ((load_hbm, load_ref), (knots_hbm, knots_ref), (start_hbm, state), (normals_hbm, normals_ref), (vol_hbm, vol_ref))
        )
    ]
    for copy in inputs:
        copy.start()
    each(blocks, lambda block: copy_of(jac_hbm, jac_buf, jac_sems, block).start())
    inputs[0].wait()
    high, middle, low = split(load_ref[...], 3)
    stacked[...] = jnp.concatenate([high, middle, high, middle, low, high], axis=0)
    for copy in inputs[1:]:
        copy.wait()

    parts = exact_sems.shape[0] // dates
    size = exact_buf.shape[1] // parts

    def sent(date, part):
        cut = pl.ds(part * size, size)
        sem = exact_sems.at[date * parts + part]
        return pltpu.make_async_copy(exact_buf.at[date, cut], exact_hbm.at[date, cut], sem)

    def zero_rates(block):
        copy_of(jac_hbm, jac_buf, jac_sems, block).wait()
        sums = jnp.sum(jac_buf[block] * knots_ref[...], axis=1, keepdims=True)
        column[pl.ds(pl.multiple_of(block * rows, rows), rows), :] = jnp.broadcast_to(sums, (rows, LANES))

    each(blocks, zero_rates)
    rate_ref[...] = column[...].T[0:1]

    def one(date):
        now = DECAY * state[...] + vol_ref[date] * normals_ref[date]
        state[...] = now
        high, middle, low = split(now, 3)
        terms = jnp.concatenate([high, high, middle, middle, high, low], axis=0)
        alive, horizon, loading = date_rows(date, knot_count)
        discount = jnp.where(alive, jnp.exp(-rate_ref[...] * horizon), 0.0)
        shift = contract(terms, stacked[...], 0, 0)
        exact = discount * jnp.exp2((-LOG2E * loading) * shift)
        exact_buf[date] = exact
        for part in range(parts):
            sent(date, part).start()
        row = pl.ds(date, 1)
        ones = jnp.ones((8, exact.shape[0]), BF16)
        feat_sum_ref[row, :] = contract(ones, exact.astype(BF16), 1, 0)[0:1]

    each(dates, one, dates)
    for part in range(parts):
        each(dates, lambda date, part=part: sent(date, part).wait())


def half_kernel(own_ref, feat_sum_ref, half_ref, terms_ref):
    knot_count, sets = half_ref.shape
    flows = own_ref[...]
    member = member_rows(flows, knot_count, sets).astype(BF16)
    half_ref[...] = contract(flows[:, :knot_count], member, 0, 0)
    terms_ref[...] = stack(feat_sum_ref[...])


def net_kernel(other_ref, half_ref, terms_ref, net_ref, out_ref):
    knot_count, sets = net_ref.shape
    flows = other_ref[...]
    member = member_rows(flows, knot_count, sets).astype(BF16)
    net = (half_ref[...] + contract(flows[:, :knot_count], member, 0, 0)).astype(BF16)
    net_ref[...] = net
    sums = folded(contract(terms_ref[...], net, 1, 0), out_ref.shape[1])
    out_ref[...] = jnp.broadcast_to(sums[None], out_ref.shape)


def value_kernel(
    own_ref, other_ref, net_ref, cpty_ref, prob_ref, exact_hbm, values_ref, rows_ref, weight_ref, flows_ref, exact_buf, sems
):
    dates = values_ref.shape[0]
    each(dates, lambda date: copy_of(exact_hbm, exact_buf, sems, date).start())
    labels = lax.broadcasted_iota(jnp.int32, (prob_ref.shape[1], cpty_ref.shape[1]), 0)
    chosen = (cpty_ref[...] == labels).astype(F32)
    weight_ref[...] = LOSS_RATE * contract(prob_ref[...], chosen, 1, 0, HIGHEST)
    sets, knot_count = rows_ref.shape
    flows_ref[...] = jnp.concatenate([own_ref[...], other_ref[...]], axis=0)
    rows = []
    for flows in (own_ref[...], other_ref[...]):
        member = member_rows(flows, knot_count, sets).astype(BF16)
        rows.append(contract(member, flows[:, :knot_count], 0, 0))
    rows_ref[...] = (rows[0] + rows[1]).astype(BF16)

    def one(date):
        copy_of(exact_hbm, exact_buf, sems, date).wait()
        values_ref[date] = contract(exact_buf[date].astype(BF16), net_ref[...], 1, 0)

    each(dates, one)


def slope_of(values, mean, base, weight):
    return weight * jax.nn.sigmoid(SHARPNESS * (values - mean + base))


def slope_kernel(paths, arrived_ref, values_ref, weight_ref, base_ref, mean_ref, sums_ref, out_ref):
    mean_ref[...] = jnp.sum(arrived_ref[...], axis=0) / paths
    for date in range(values_ref.shape[0]):
        row = slice(date, date + 1)
        slope = slope_of(values_ref[date], mean_ref[row, :], base_ref[row, :], weight_ref[row, :])
        sums_ref[row, :] = jnp.sum(slope, axis=0, keepdims=True)
    out_ref[...] = jnp.broadcast_to(sums_ref[...][None], out_ref.shape)


def adjoint_kernel(
    mean_ref, sums_ref, weight_ref, base_ref, feat_sum_ref, values_ref, net_ref, flows_ref, exact_hbm,
    blend_ref, rate_ref, trades_ref, cross_ref, exact_buf, sems, rate, loads,
):
    dates = values_ref.shape[0]
    paths, knot_count = blend_ref.shape
    each(dates, lambda date: copy_of(exact_hbm, exact_buf, sems, date).start())
    blend_ref[...] = jnp.zeros_like(blend_ref)
    rate[...] = jnp.zeros_like(rate)
    loads[...] = jnp.zeros_like(loads)
    flows = flows_ref[...]
    member = member_rows(flows, knot_count, net_ref.shape[0])
    flows = flows[:, :knot_count]
    cross_ref[...] = folded(contract(stack(feat_sum_ref[...]), flows, 1, 1), dates)

    def one(date):
        _, horizon, loading = date_rows(date, knot_count)
        factor = loading * jnp.exp(-MEAN_REV * STEP_YEARS * (date + 1).astype(F32))
        row = pl.ds(date, 1)
        slope = slope_of(values_ref[date], mean_ref[row, :], base_ref[row, :], weight_ref[row, :])
        adjoint = (slope - sums_ref[row, :] / paths).astype(BF16)
        copy_of(exact_hbm, exact_buf, sems, date).wait()
        exact = exact_buf[date]
        product = contract(adjoint, net_ref[...], 1, 0) * exact
        blend_ref[...] += factor * product
        rate[...] += horizon * jnp.sum(product.reshape(-1, 8, knot_count), axis=0)
        loads[...] += contract(adjoint, exact.astype(BF16), 0, 0)

    each(dates, one, 2 - dates % 2)
    shares = jnp.zeros(member.shape, F32)
    for part in split(loads[...], 3):
        shares = shares + contract(flows, part, 1, 1)
    trades_ref[...] = jnp.sum(jnp.where(member, shares, 0.0).T, axis=0, keepdims=True)
    rate_ref[...] = jnp.sum(rate[...], axis=0, keepdims=True)


def finish_kernel(
    paths, local, parity_ref, arrived_ref, sums_ref, feat_sum_ref, net_ref, flows_ref, rate_ref, trades_ref, cross_ref,
    shift_ref, out_ref,
):
    sets, knot_count = net_ref.shape
    gap = sums_ref[...] / local - jnp.sum(arrived_ref[...], axis=0) / paths
    flows = flows_ref[...]
    member = member_rows(flows, knot_count, sets).astype(BF16)
    terms = stack(gap)
    spread = folded(contract(terms, member, 1, 1), gap.shape[0])
    adjoint = folded(contract(terms, net_ref[...], 1, 0), gap.shape[0])
    total = rate_ref[...]
    for date in range(shift_ref.shape[0]):
        row = slice(date, date + 1)
        _, horizon, loading = date_rows(jnp.int32(date), knot_count)
        shift_ref[row, :] = loading * math.exp(-MEAN_REV * STEP_YEARS * (date + 1)) * adjoint[row]
        total = total + horizon * adjoint[row] * feat_sum_ref[row, :]
    trades = trades_ref[...] + jnp.sum(spread * cross_ref[...], axis=0, keepdims=True)
    count = trades.shape[1]
    trades = pltpu.roll(jnp.broadcast_to(trades, (8, count)), parity_ref[0] * (count // 2), 1)[0:1]
    shards, _, width = out_ref.shape
    pad = jnp.zeros((1, width - knot_count - trades.shape[1]), F32)
    row = jnp.concatenate([-total / paths, pad, trades / paths], axis=1)
    out_ref[...] = jnp.broadcast_to(row[None], out_ref.shape)


def start_kernel(
    blend_ref, shift_ref, load_ref, later_ref, exact_hbm, jac_hbm, out_ref, kept_ref, exact_buf, sems, jac_sems, blend
):
    dates = shift_ref.shape[0]
    kept = kept_ref.shape[0]
    each(dates, lambda date: copy_of(exact_hbm, exact_buf, sems, date).start())
    each(kept, lambda block: copy_of(jac_hbm, kept_ref, jac_sems, block).start())
    blend[...] = blend_ref[...]

    def one(date):
        copy_of(exact_hbm, exact_buf, sems, date).wait()
        blend[...] += shift_ref[pl.ds(date, 1), :] * exact_buf[date]

    each(dates, one)
    carried = contract(load_ref[...], blend[...], 1, 1, HIGHEST)
    out_ref[...] = math.exp(-MEAN_REV * STEP_YEARS * dates) * later_ref[...] - carried
    each(kept, lambda block: copy_of(jac_hbm, kept_ref, jac_sems, block).wait())


def final_kernel(index_ref, arrived_ref, kept_ref, jac_hbm, knot_ref, alloc_ref, jac_buf, sems, column, total):
    blocks, rows, knot_count = jac_hbm.shape
    kept = kept_ref.shape[0]
    missing = blocks - kept

    def fetched(block):
        return pltpu.make_async_copy(jac_hbm.at[kept + block], jac_buf.at[block], sems.at[block])

    each(missing, lambda block: fetched(block).start())
    row = jnp.sum(arrived_ref[...], axis=0)
    trades = alloc_ref.shape[1]
    parts = row[:, round_up(knot_count, LANES) :]
    count = parts.shape[1]
    offset = index_ref[0]
    parts = jnp.broadcast_to(parts, (8, count))
    alloc_ref[...] = pltpu.roll(parts, lax.rem(count - offset, count), 1)[0:1, :trades]
    column[...] = jnp.broadcast_to(row[:, :knot_count], (LANES, knot_count)).T
    total[...] = jnp.zeros_like(total)

    def add(source, block, first_block):
        part = column[pl.ds(pl.multiple_of((first_block + block) * rows, rows), rows), :]
        for first in range(0, knot_count, LANES):
            size = min(LANES, knot_count - first)
            cut = slice(first, first + size)
            scaled = source[block, :, cut] * part[:, :size]
            total[:, cut] += jnp.sum(scaled.reshape(-1, total.shape[0], size), axis=0)

    def late(block):
        fetched(block).wait()
        add(jac_buf, block, kept)

    each(kept, lambda block: add(kept_ref, block, 0))
    each(missing, late)
    knot_ref[...] = jnp.sum(total[...], axis=0, keepdims=True)


VMEM = pl.BlockSpec(memory_space=pltpu.VMEM)
SMEM = pl.BlockSpec(memory_space=pltpu.SMEM)


def shaped(shape, dtype=F32):
    return jax.ShapeDtypeStruct(shape, dtype)


def held(array):
    size = array.dtype.itemsize
    rows = array.shape[-2] if len(array.shape) > 1 else 1
    lead = math.prod(array.shape[:-2])
    return lead * round_up(rows, 8) * round_up(array.shape[-1], LANES) * size


def run(name, kernel, out_shape, operands, scalars=0, hbm=(), scratch=(), copies=(), buffers=1, smem=(), flops=0, grant=0):
    arrays = list(operands) + list(out_shape)
    room = sum(held(array) for array in scratch) + (8 << 20)
    specs = []
    for place, array in enumerate(arrays):
        if place < scalars:
            specs.append(SMEM)
        elif place in hbm:
            specs.append(pl.BlockSpec(memory_space=pltpu.HBM))
        else:
            specs.append(VMEM)
            room += held(array)
    moved = sum(held(array) for array in arrays)
    return pl.pallas_call(
        kernel,
        out_shape=tuple(out_shape),
        in_specs=specs[: len(operands)],
        out_specs=tuple(specs[len(operands) :]),
        scratch_shapes=[pltpu.VMEM(array.shape, array.dtype) for array in scratch[:buffers]]
        + [pltpu.SemaphoreType.DMA((count,)) for count in copies]
        + [pltpu.VMEM(array.shape, array.dtype) for array in scratch[buffers:]]
        + [pltpu.SMEM(array.shape, array.dtype) for array in smem],
        compiler_params=pltpu.CompilerParams(vmem_limit_bytes=grant or room),
        cost_estimate=pl.CostEstimate(flops=flops, bytes_accessed=moved, transcendentals=0),
        name=name,
    )(*operands)


def per_device(
    normals,
    start_state,
    later_adjoint,
    vol,
    factor_load,
    knots,
    spline_jac,
    cashflows,
    trade_set,
    trade_end,
    set_cpty,
    default_prob,
    base_value,
):
    dates, factors, paths = normals.shape
    knot_count = knots.shape[0]
    sets = base_value.shape[1]
    shards = lax.axis_size("path")
    trades = cashflows.shape[0]
    all_trades = trades * shards
    all_paths = paths * shards
    width = round_up(knot_count + 2, LANES)
    work = 2 * dates * paths * knot_count
    grid_rows = shaped((dates, knot_count))
    set_rows = shaped((dates, sets))
    set_copies = shaped((shards, dates, sets))

    (copies,) = run(
        "prep",
        prep_kernel,
        [shaped((shards // 2, trades, width), BF16)],
        [trade_end, trade_set.reshape(trades), cashflows],
        scalars=2,
        grant=LARGE,
    )
    pairs = shards // 2
    places = [(2 * pairs - 1 - pair - pairs // 2) % pairs for pair in range(pairs)]
    own = exchange(copies, [[2 * pair + side for pair in places] for side in range(2)])
    own = own.reshape(all_trades // 2, width)
    index = lax.axis_index("path").astype(jnp.int32)
    parity = lax.rem(index, 2)
    place = lax.rem(2 * pairs - 1 - lax.div(index, 2) - pairs // 2, pairs)
    offset = parity * (all_trades // 2) + place * trades
    blocks = next(count for count in (8, 4, 2, 1) if knot_count % (8 * count) == 0)
    jac_blocks = spline_jac.reshape(blocks, knot_count // blocks, knot_count)

    exact, feat_sums = run(
        "features",
        feature_kernel,
        [shaped((dates, paths, knot_count)), grid_rows],
        [vol, normals, start_state, factor_load, knots.reshape(1, knot_count), jac_blocks],
        hbm=(0, 1, 2, 3, 4, 5, 6),
        scratch=[
            shaped((dates, paths, knot_count)),
            shaped(jac_blocks.shape),
            shaped(normals.shape),
            shaped(start_state.shape),
            shaped(factor_load.shape),
            shaped((1, knot_count)),
            shaped((6 * factors, knot_count), BF16),
            shaped((knot_count, LANES)),
            shaped((1, knot_count)),
        ],
        buffers=2,
        copies=(dates * (4 if paths % 64 == 0 else 1), blocks, 5),
        smem=(shaped(vol.shape),),
        flops=6 * factors * work,
        grant=LARGE,
    )

    own, feat_sums = lax.optimization_barrier((own, feat_sums))
    other = lax.ppermute(own, "path", [(shard, shard ^ 1) for shard in range(shards)])
    half, terms = run(
        "half",
        half_kernel,
        [shaped((knot_count, sets)), shaped((3 * dates, knot_count), BF16)],
        [own, feat_sums],
        flops=sets * all_trades * knot_count,
    )
    net_columns, copies = run(
        "net",
        net_kernel,
        [shaped((knot_count, sets), BF16), set_copies],
        [other, half, terms],
        flops=sets * all_trades * knot_count,
    )
    arrived = exchange(copies, [list(range(shards))[::-1]])
    values, net_rows, weight, flows = run(
        "values",
        value_kernel,
        [shaped((dates, paths, sets)), shaped((sets, knot_count), BF16), set_rows, shaped((all_trades, width), BF16)],
        [own, other, net_columns, set_cpty.reshape(1, sets), default_prob, exact],
        hbm=(5,),
        scratch=[shaped((dates, paths, knot_count))],
        copies=(dates,),
        flops=sets * work,
        grant=MIDDLE,
    )
    mean, slope_sums, copies = run(
        "slopes",
        functools.partial(slope_kernel, all_paths),
        [set_rows, set_rows, set_copies],
        [arrived, values, weight, base_value],
        flops=16 * dates * paths * sets,
    )
    arrived = exchange(copies, [list(range(shards))[::-1]])
    blend, rate, trade_parts, cross = run(
        "adjoint",
        adjoint_kernel,
        [
            shaped((paths, knot_count)),
            shaped((1, knot_count)),
            shaped((1, all_trades)),
            shaped((dates, all_trades)),
        ],
        [mean, slope_sums, weight, base_value, feat_sums, values, net_rows, flows, exact],
        hbm=(8,),
        scratch=[
            shaped((dates, paths, knot_count)),
            shaped((8, knot_count)),
            shaped((sets, knot_count)),
        ],
        copies=(dates,),
        flops=2 * sets * work,
        grant=MIDDLE,
    )
    row_width = round_up(knot_count, LANES) + all_trades
    shift, copies = run(
        "finish",
        functools.partial(finish_kernel, all_paths, paths),
        [grid_rows, shaped((shards, 1, row_width))],
        [parity.reshape(1), arrived, slope_sums, feat_sums, net_rows, flows, rate, trade_parts, cross],
        scalars=1,
        flops=6 * sets * dates * knot_count,
    )
    arrived = exchange(copies, [list(range(shards))[::-1]])
    kept = blocks * 4 // 8
    start_adjoint, kept_blocks = run(
        "start",
        start_kernel,
        [shaped((factors, paths)), shaped((kept,) + jac_blocks.shape[1:])],
        [blend, shift, factor_load, later_adjoint, exact, jac_blocks],
        hbm=(4, 5),
        scratch=[shaped((dates, paths, knot_count)), shaped((paths, knot_count))],
        copies=(dates, kept),
        flops=2 * factors * paths * knot_count,
        grant=49<<20,
    )
    knot_grad, alloc = run(
        "final",
        final_kernel,
        [shaped((1, knot_count)), shaped((1, trades))],
        [offset.reshape(1), arrived, kept_blocks, jac_blocks],
        scalars=1,
        hbm=(3,),
        scratch=[
            shaped((blocks - kept,) + jac_blocks.shape[1:]),
            shaped((knot_count, LANES)),
            shaped((8, knot_count)),
        ],
        copies=(blocks - kept,),
        flops=2 * knot_count**2,
        grant=51<<20,
    )
    return knot_grad.reshape(knot_count), alloc.reshape(trades), start_adjoint


def solution(mesh):
    in_specs = (
        P(None, None, ("group", "path")),
        P(None, ("group", "path")),
        P(None, ("group", "path")),
        P(),
        P(),
        P(),
        P(),
        P(("group", "path"), None),
        P(("group", "path"), None),
        P(("group", "path")),
        P("group", None),
        P(),
        P(None, "group"),
    )
    out_specs = (P("group"), P(("group", "path")), P(None, ("group", "path")))
    return jax.shard_map(
        per_device, mesh=mesh, in_specs=in_specs, out_specs=out_specs, check_vma=False
    )
```

```python
import functools
import math

import jax
import jax.numpy as jnp
from jax import lax
from jax.experimental import pallas as pl
from jax.experimental.pallas import tpu as pltpu
from jax.sharding import PartitionSpec as P

MEAN_REV = 0.05
STEP_YEARS = 0.25
HORIZON_YEARS = 30.0
SHARPNESS = 4.0
LOSS_RATE = 0.6
BASE = 128
LANES = 128
LARGE = 58 << 20
MIDDLE = 50 << 20
LOG2E = math.log2(math.e)
DECAY = math.exp(-MEAN_REV * STEP_YEARS)
HIGHEST = lax.Precision.HIGHEST
F32 = jnp.float32
BF16 = jnp.bfloat16


def round_up(size, step):
    return -(-size // step) * step


def exchange(copies, groups=None):
    return lax.all_to_all(copies, "path", 0, 0, axis_index_groups=groups)


def split(value, terms):
    parts = []
    for _ in range(terms):
        part = value.astype(BF16)
        parts.append(part)
        value = value - part.astype(F32)
    return parts


def contract(lhs, rhs, lhs_dim, rhs_dim, precision=None):
    return lax.dot_general(
        lhs,
        rhs,
        (((lhs_dim,), (rhs_dim,)), ((), ())),
        precision=precision,
        preferred_element_type=F32,
    )


def folded(parts, rows):
    total = parts[:rows]
    for first in range(rows, parts.shape[0], rows):
        total = total + parts[first : first + rows]
    return total


def stack(value):
    return jnp.concatenate(split(value, 3), axis=0)


def each(count, body, group=1):
    def step(index, carry):
        for offset in range(group):
            body(index * group + offset)
        return carry

    lax.fori_loop(0, count // group, step, 0)


def copy_of(source, target, sems, index):
    return pltpu.make_async_copy(source.at[index], target.at[index], sems.at[index])


def date_rows(date, knot_count):
    point = lax.broadcasted_iota(jnp.int32, (1, knot_count), 1) + 1
    alive = 120 * point > knot_count * (date + 1)
    maturity = HORIZON_YEARS * point.astype(F32) / knot_count
    fixing = STEP_YEARS * (date + 1).astype(F32)
    horizon = jnp.where(alive, maturity - fixing, 0.0)
    loading = (1.0 - jnp.exp(-MEAN_REV * horizon)) / MEAN_REV
    return alive, horizon, loading


def member_rows(flows, knot_count, set_count):
    digits = flows[:, knot_count : knot_count + 2].astype(F32)
    sets = (digits[:, 0:1] * BASE + digits[:, 1:2]).astype(jnp.int32)
    labels = lax.broadcasted_iota(jnp.int32, (flows.shape[0], set_count), 1)
    return sets == labels


def prep_kernel(end_ref, set_ref, cash_ref, out_ref):
    shards, trades, width = out_ref.shape
    knot_count = cash_ref.shape[1]
    row = lax.broadcasted_iota(jnp.int32, (trades, width), 0)
    point = lax.broadcasted_iota(jnp.int32, (trades, width), 1)
    ends = jnp.zeros((trades, width), jnp.int32)
    sets = jnp.zeros((trades, width), jnp.int32)
    for trade in range(trades):
        ends = jnp.where(row == trade, end_ref[trade], ends)
        sets = jnp.where(row == trade, set_ref[trade], sets)
    cash = jnp.concatenate(
        [cash_ref[...].astype(F32), jnp.zeros((trades, width - knot_count), F32)], axis=1
    )
    high = lax.shift_right_logical(sets, BASE.bit_length() - 1)
    low = sets & (BASE - 1)
    flows = jnp.where(point < jnp.minimum(ends, knot_count), cash, 0.0)
    flows = jnp.where(point == knot_count, high.astype(F32), flows)
    flows = jnp.where(point == knot_count + 1, low.astype(F32), flows).astype(BF16)
    for shard in range(shards):
        out_ref[shard] = flows


def feature_kernel(
    vol_hbm, normals_hbm, start_hbm, load_hbm, knots_hbm, jac_hbm,
    exact_hbm, feat_sum_ref,
    exact_buf, jac_buf, exact_sems, jac_sems, sems, normals_ref, state, load_ref, knots_ref, stacked, column, rate_ref, vol_ref,
):
    dates = normals_ref.shape[0]
    blocks, rows, knot_count = jac_hbm.shape
    inputs = [
        pltpu.make_async_copy(source, target, sems.at[place])
        for place, (source, target) in enumerate(
            ((load_hbm, load_ref), (knots_hbm, knots_ref), (start_hbm, state), (normals_hbm, normals_ref), (vol_hbm, vol_ref))
        )
    ]
    for copy in inputs:
        copy.start()
    each(blocks, lambda block: copy_of(jac_hbm, jac_buf, jac_sems, block).start())
    inputs[0].wait()
    high, middle, low = split(load_ref[...], 3)
    stacked[...] = jnp.concatenate([high, middle, high, middle, low, high], axis=0)
    for copy in inputs[1:]:
        copy.wait()

    parts = exact_sems.shape[0] // dates
    size = exact_buf.shape[1] // parts

    def sent(date, part):
        cut = pl.ds(part * size, size)
        sem = exact_sems.at[date * parts + part]
        return pltpu.make_async_copy(exact_buf.at[date, cut], exact_hbm.at[date, cut], sem)

    def zero_rates(block):
        copy_of(jac_hbm, jac_buf, jac_sems, block).wait()
        sums = jnp.zeros((rows, LANES), F32)
        for first in range(0, knot_count, LANES):
            size = min(LANES, knot_count - first)
            cut = slice(first, first + size)
            part = jac_buf[block, :, cut] * knots_ref[:, cut]
            if size < LANES:
                part = jnp.concatenate([part, jnp.zeros((rows, LANES - size), F32)], axis=1)
            sums = sums + part
        column[pl.ds(pl.multiple_of(block * rows, rows), rows), :] = sums

    each(blocks, zero_rates)
    rate_ref[...] = jnp.sum(column[...].T, axis=0, keepdims=True)

    def one(date):
        now = DECAY * state[...] + vol_ref[date] * normals_ref[date]
        state[...] = now
        high, middle, low = split(now, 3)
        terms = jnp.concatenate([high, high, middle, middle, high, low], axis=0)
        alive, horizon, loading = date_rows(date, knot_count)
        discount = jnp.where(alive, jnp.exp(-rate_ref[...] * horizon), 0.0)
        shift = contract(terms, stacked[...], 0, 0)
        exact = discount * jnp.exp2((-LOG2E * loading) * shift)
        exact_buf[date] = exact
        for part in range(parts):
            sent(date, part).start()
        row = pl.ds(date, 1)
        feat_sum_ref[row, :] = jnp.sum(exact.astype(BF16).astype(F32), axis=0, keepdims=True)

    each(dates, one, dates)
    for part in range(parts):
        each(dates, lambda date, part=part: sent(date, part).wait())


def half_kernel(own_ref, feat_sum_ref, half_ref, terms_ref):
    knot_count, sets = half_ref.shape
    flows = own_ref[...]
    member = member_rows(flows, knot_count, sets).astype(BF16)
    half_ref[...] = contract(flows[:, :knot_count], member, 0, 0)
    terms_ref[...] = stack(feat_sum_ref[...])


def net_kernel(own_ref, other_ref, half_ref, terms_ref, flows_ref, net_ref, out_ref):
    knot_count, sets = net_ref.shape
    flows_ref[...] = jnp.concatenate([own_ref[...], other_ref[...]], axis=0)
    flows = other_ref[...]
    member = member_rows(flows, knot_count, sets).astype(BF16)
    net = (half_ref[...] + contract(flows[:, :knot_count], member, 0, 0)).astype(BF16)
    net_ref[...] = net
    sums = folded(contract(terms_ref[...], net, 1, 0), out_ref.shape[1])
    out_ref[...] = jnp.broadcast_to(sums[None], out_ref.shape)


def value_kernel(
    flows_ref, net_ref, cpty_ref, prob_ref, exact_hbm, values_ref, rows_ref, weight_ref, exact_buf, sems
):
    dates = values_ref.shape[0]
    each(dates, lambda date: copy_of(exact_hbm, exact_buf, sems, date).start())
    labels = lax.broadcasted_iota(jnp.int32, (prob_ref.shape[1], cpty_ref.shape[1]), 0)
    chosen = (cpty_ref[...] == labels).astype(F32)
    weight_ref[...] = LOSS_RATE * contract(prob_ref[...], chosen, 1, 0, HIGHEST)
    sets, knot_count = rows_ref.shape
    half = flows_ref.shape[0] // 2
    rows = []
    for first in (0, half):
        flows = flows_ref[first : first + half, :]
        member = member_rows(flows, knot_count, sets).astype(BF16)
        rows.append(contract(member, flows[:, :knot_count], 0, 0))
    rows_ref[...] = (rows[0] + rows[1]).astype(BF16)

    def one(date):
        copy_of(exact_hbm, exact_buf, sems, date).wait()
        values_ref[date] = contract(exact_buf[date].astype(BF16), net_ref[...], 1, 0)

    each(dates, one)


def slope_of(values, mean, base, weight):
    return weight * jax.nn.sigmoid(SHARPNESS * (values - mean + base))


def slope_kernel(paths, arrived_ref, values_ref, weight_ref, base_ref, mean_ref, sums_ref, out_ref):
    mean_ref[...] = jnp.sum(arrived_ref[...], axis=0) / paths
    for date in range(values_ref.shape[0]):
        row = slice(date, date + 1)
        slope = slope_of(values_ref[date], mean_ref[row, :], base_ref[row, :], weight_ref[row, :])
        sums_ref[row, :] = jnp.sum(slope, axis=0, keepdims=True)
    out_ref[...] = jnp.broadcast_to(sums_ref[...][None], out_ref.shape)


def adjoint_kernel(
    mean_ref, sums_ref, weight_ref, base_ref, feat_sum_ref, values_ref, net_ref, flows_ref, exact_hbm,
    blend_ref, rate_ref, trades_ref, cross_ref, exact_buf, sems, rate, loads,
):
    dates = values_ref.shape[0]
    paths, knot_count = blend_ref.shape
    each(dates, lambda date: copy_of(exact_hbm, exact_buf, sems, date).start())
    blend_ref[...] = jnp.zeros_like(blend_ref)
    rate[...] = jnp.zeros_like(rate)
    loads[...] = jnp.zeros_like(loads)
    flows = flows_ref[...]
    member = member_rows(flows, knot_count, net_ref.shape[0])
    flows = flows[:, :knot_count]
    cross_ref[...] = folded(contract(stack(feat_sum_ref[...]), flows, 1, 1), dates)

    def one(date):
        _, horizon, loading = date_rows(date, knot_count)
        factor = loading * jnp.exp(-MEAN_REV * STEP_YEARS * (date + 1).astype(F32))
        row = pl.ds(date, 1)
        slope = slope_of(values_ref[date], mean_ref[row, :], base_ref[row, :], weight_ref[row, :])
        adjoint = (slope - sums_ref[row, :] / paths).astype(BF16)
        copy_of(exact_hbm, exact_buf, sems, date).wait()
        exact = exact_buf[date]
        product = contract(adjoint, net_ref[...], 1, 0) * exact
        blend_ref[...] += factor * product
        rate[...] += horizon * jnp.sum(product.reshape(-1, 8, knot_count), axis=0)
        loads[...] += contract(adjoint, exact.astype(BF16), 0, 0)

    each(dates, one, 2 - dates % 2)
    shares = jnp.zeros(member.shape, F32)
    for part in split(loads[...], 3):
        shares = shares + contract(flows, part, 1, 1)
    trades_ref[...] = jnp.sum(jnp.where(member, shares, 0.0).T, axis=0, keepdims=True)
    rate_ref[...] = jnp.sum(rate[...], axis=0, keepdims=True)


def finish_kernel(
    paths, local, parity_ref, arrived_ref, sums_ref, feat_sum_ref, net_ref, flows_ref, rate_ref, trades_ref, cross_ref,
    shift_ref, out_ref,
):
    sets, knot_count = net_ref.shape
    gap = sums_ref[...] / local - jnp.sum(arrived_ref[...], axis=0) / paths
    flows = flows_ref[...]
    member = member_rows(flows, knot_count, sets).astype(BF16)
    terms = stack(gap)
    spread = folded(contract(terms, member, 1, 1), gap.shape[0])
    adjoint = folded(contract(terms, net_ref[...], 1, 0), gap.shape[0])
    total = rate_ref[...]
    for date in range(shift_ref.shape[0]):
        row = slice(date, date + 1)
        _, horizon, loading = date_rows(jnp.int32(date), knot_count)
        shift_ref[row, :] = loading * math.exp(-MEAN_REV * STEP_YEARS * (date + 1)) * adjoint[row]
        total = total + horizon * adjoint[row] * feat_sum_ref[row, :]
    trades = trades_ref[...] + jnp.sum(spread * cross_ref[...], axis=0, keepdims=True)
    count = trades.shape[1]
    trades = pltpu.roll(jnp.broadcast_to(trades, (8, count)), parity_ref[0] * (count // 2), 1)[0:1]
    shards, _, width = out_ref.shape
    pad = jnp.zeros((1, width - knot_count - trades.shape[1]), F32)
    row = jnp.concatenate([-total / paths, pad, trades / paths], axis=1)
    out_ref[...] = jnp.broadcast_to(row[None], out_ref.shape)


def start_kernel(
    blend_ref, shift_ref, load_ref, later_ref, exact_hbm, jac_hbm, out_ref, kept_ref, exact_buf, sems, jac_sems, blend
):
    dates = shift_ref.shape[0]
    kept = kept_ref.shape[0]
    each(dates, lambda date: copy_of(exact_hbm, exact_buf, sems, date).start())
    each(kept, lambda block: copy_of(jac_hbm, kept_ref, jac_sems, block).start())
    blend[...] = blend_ref[...]

    def one(date):
        copy_of(exact_hbm, exact_buf, sems, date).wait()
        blend[...] += shift_ref[pl.ds(date, 1), :] * exact_buf[date]

    each(dates, one)
    carried = contract(load_ref[...], blend[...], 1, 1, HIGHEST)
    out_ref[...] = math.exp(-MEAN_REV * STEP_YEARS * dates) * later_ref[...] - carried
    each(kept, lambda block: copy_of(jac_hbm, kept_ref, jac_sems, block).wait())


def final_kernel(index_ref, arrived_ref, kept_ref, jac_hbm, knot_ref, alloc_ref, jac_buf, sems, column, total):
    blocks, rows, knot_count = jac_hbm.shape
    kept = kept_ref.shape[0]
    missing = blocks - kept

    def fetched(block):
        return pltpu.make_async_copy(jac_hbm.at[kept + block], jac_buf.at[block], sems.at[block])

    each(missing, lambda block: fetched(block).start())
    row = jnp.sum(arrived_ref[...], axis=0)
    trades = alloc_ref.shape[1]
    parts = row[:, round_up(knot_count, LANES) :]
    count = parts.shape[1]
    offset = index_ref[0]
    parts = jnp.broadcast_to(parts, (8, count))
    alloc_ref[...] = pltpu.roll(parts, lax.rem(count - offset, count), 1)[0:1, :trades]
    column[...] = jnp.broadcast_to(row[:, :knot_count], (LANES, knot_count)).T
    total[...] = jnp.zeros_like(total)

    def add(source, block, first_block):
        part = column[pl.ds(pl.multiple_of((first_block + block) * rows, rows), rows), :]
        for first in range(0, knot_count, LANES):
            size = min(LANES, knot_count - first)
            cut = slice(first, first + size)
            scaled = source[block, :, cut] * part[:, :size]
            total[:, cut] += jnp.sum(scaled.reshape(-1, total.shape[0], size), axis=0)

    def late(block):
        fetched(block).wait()
        add(jac_buf, block, kept)

    each(kept, lambda block: add(kept_ref, block, 0))
    each(missing, late)
    knot_ref[...] = jnp.sum(total[...], axis=0, keepdims=True)


VMEM = pl.BlockSpec(memory_space=pltpu.VMEM)
SMEM = pl.BlockSpec(memory_space=pltpu.SMEM)


def shaped(shape, dtype=F32):
    return jax.ShapeDtypeStruct(shape, dtype)


def held(array):
    size = array.dtype.itemsize
    rows = array.shape[-2] if len(array.shape) > 1 else 1
    lead = math.prod(array.shape[:-2])
    return lead * round_up(rows, 8) * round_up(array.shape[-1], LANES) * size


def run(name, kernel, out_shape, operands, scalars=0, hbm=(), scratch=(), copies=(), buffers=1, smem=(), flops=0, grant=0):
    arrays = list(operands) + list(out_shape)
    room = sum(held(array) for array in scratch) + (8 << 20)
    specs = []
    for place, array in enumerate(arrays):
        if place < scalars:
            specs.append(SMEM)
        elif place in hbm:
            specs.append(pl.BlockSpec(memory_space=pltpu.HBM))
        else:
            specs.append(VMEM)
            room += held(array)
    moved = sum(held(array) for array in arrays)
    return pl.pallas_call(
        kernel,
        out_shape=tuple(out_shape),
        in_specs=specs[: len(operands)],
        out_specs=tuple(specs[len(operands) :]),
        scratch_shapes=[pltpu.VMEM(array.shape, array.dtype) for array in scratch[:buffers]]
        + [pltpu.SemaphoreType.DMA((count,)) for count in copies]
        + [pltpu.VMEM(array.shape, array.dtype) for array in scratch[buffers:]]
        + [pltpu.SMEM(array.shape, array.dtype) for array in smem],
        compiler_params=pltpu.CompilerParams(vmem_limit_bytes=grant or room),
        cost_estimate=pl.CostEstimate(flops=flops, bytes_accessed=moved, transcendentals=0),
        name=name,
    )(*operands)


def per_device(
    normals,
    start_state,
    later_adjoint,
    vol,
    factor_load,
    knots,
    spline_jac,
    cashflows,
    trade_set,
    trade_end,
    set_cpty,
    default_prob,
    base_value,
):
    dates, factors, paths = normals.shape
    knot_count = knots.shape[0]
    sets = base_value.shape[1]
    shards = lax.axis_size("path")
    trades = cashflows.shape[0]
    all_trades = trades * shards
    all_paths = paths * shards
    width = round_up(knot_count + 2, LANES)
    work = 2 * dates * paths * knot_count
    grid_rows = shaped((dates, knot_count))
    set_rows = shaped((dates, sets))
    set_copies = shaped((shards, dates, sets))

    (copies,) = run(
        "prep",
        prep_kernel,
        [shaped((shards // 2, trades, width), BF16)],
        [trade_end, trade_set.reshape(trades), cashflows],
        scalars=2,
        grant=LARGE,
    )
    pairs = shards // 2
    places = [(2 * pairs - 1 - pair - pairs // 2) % pairs for pair in range(pairs)]
    own = exchange(copies, [[2 * pair + side for pair in places] for side in range(2)])
    own = own.reshape(all_trades // 2, width)
    index = lax.axis_index("path").astype(jnp.int32)
    parity = lax.rem(index, 2)
    place = lax.rem(2 * pairs - 1 - lax.div(index, 2) - pairs // 2, pairs)
    offset = parity * (all_trades // 2) + place * trades
    blocks = next(count for count in (8, 4, 2, 1) if knot_count % (8 * count) == 0)
    jac_blocks = spline_jac.reshape(blocks, knot_count // blocks, knot_count)

    exact, feat_sums = run(
        "features",
        feature_kernel,
        [shaped((dates, paths, knot_count)), grid_rows],
        [vol, normals, start_state, factor_load, knots.reshape(1, knot_count), jac_blocks],
        hbm=(0, 1, 2, 3, 4, 5, 6),
        scratch=[
            shaped((dates, paths, knot_count)),
            shaped(jac_blocks.shape),
            shaped(normals.shape),
            shaped(start_state.shape),
            shaped(factor_load.shape),
            shaped((1, knot_count)),
            shaped((6 * factors, knot_count), BF16),
            shaped((knot_count, LANES)),
            shaped((1, knot_count)),
        ],
        buffers=2,
        copies=(dates * (4 if paths % 64 == 0 else 1), blocks, 5),
        smem=(shaped(vol.shape),),
        flops=6 * factors * work,
        grant=LARGE,
    )

    own, feat_sums = lax.optimization_barrier((own, feat_sums))
    other = lax.ppermute(own, "path", [(shard, shard ^ 1) for shard in range(shards)])
    half, terms = run(
        "half",
        half_kernel,
        [shaped((knot_count, sets)), shaped((3 * dates, knot_count), BF16)],
        [own, feat_sums],
        flops=sets * all_trades * knot_count,
    )
    flows, net_columns, copies = run(
        "net",
        net_kernel,
        [shaped((all_trades, width), BF16), shaped((knot_count, sets), BF16), set_copies],
        [own, other, half, terms],
        flops=sets * all_trades * knot_count,
    )
    arrived = exchange(copies, [list(range(shards))[::-1]])
    values, net_rows, weight = run(
        "values",
        value_kernel,
        [shaped((dates, paths, sets)), shaped((sets, knot_count), BF16), set_rows],
        [flows, net_columns, set_cpty.reshape(1, sets), default_prob, exact],
        hbm=(4,),
        scratch=[shaped((dates, paths, knot_count))],
        copies=(dates,),
        flops=sets * work,
        grant=MIDDLE,
    )
    mean, slope_sums, copies = run(
        "slopes",
        functools.partial(slope_kernel, all_paths),
        [set_rows, set_rows, set_copies],
        [arrived, values, weight, base_value],
        flops=16 * dates * paths * sets,
    )
    arrived = exchange(copies, [list(range(shards))[::-1]])
    blend, rate, trade_parts, cross = run(
        "adjoint",
        adjoint_kernel,
        [
            shaped((paths, knot_count)),
            shaped((1, knot_count)),
            shaped((1, all_trades)),
            shaped((dates, all_trades)),
        ],
        [mean, slope_sums, weight, base_value, feat_sums, values, net_rows, flows, exact],
        hbm=(8,),
        scratch=[
            shaped((dates, paths, knot_count)),
            shaped((8, knot_count)),
            shaped((sets, knot_count)),
        ],
        copies=(dates,),
        flops=2 * sets * work,
        grant=MIDDLE,
    )
    row_width = round_up(knot_count, LANES) + all_trades
    shift, copies = run(
        "finish",
        functools.partial(finish_kernel, all_paths, paths),
        [grid_rows, shaped((shards, 1, row_width))],
        [parity.reshape(1), arrived, slope_sums, feat_sums, net_rows, flows, rate, trade_parts, cross],
        scalars=1,
        flops=6 * sets * dates * knot_count,
    )
    arrived = exchange(copies, [list(range(shards))[::-1]])
    kept = blocks * 4 // 8
    start_adjoint, kept_blocks = run(
        "start",
        start_kernel,
        [shaped((factors, paths)), shaped((kept,) + jac_blocks.shape[1:])],
        [blend, shift, factor_load, later_adjoint, exact, jac_blocks],
        hbm=(4, 5),
        scratch=[shaped((dates, paths, knot_count)), shaped((paths, knot_count))],
        copies=(dates, kept),
        flops=2 * factors * paths * knot_count,
        grant=49<<20,
    )
    knot_grad, alloc = run(
        "final",
        final_kernel,
        [shaped((1, knot_count)), shaped((1, trades))],
        [offset.reshape(1), arrived, kept_blocks, jac_blocks],
        scalars=1,
        hbm=(3,),
        scratch=[
            shaped((blocks - kept,) + jac_blocks.shape[1:]),
            shaped((knot_count, LANES)),
            shaped((8, knot_count)),
        ],
        copies=(blocks - kept,),
        flops=2 * knot_count**2,
        grant=51<<20,
    )
    return knot_grad.reshape(knot_count), alloc.reshape(trades), start_adjoint


def solution(mesh):
    in_specs = (
        P(None, None, ("group", "path")),
        P(None, ("group", "path")),
        P(None, ("group", "path")),
        P(),
        P(),
        P(),
        P(),
        P(("group", "path"), None),
        P(("group", "path"), None),
        P(("group", "path")),
        P("group", None),
        P(),
        P(None, "group"),
    )
    out_specs = (P("group"), P(("group", "path")), P(None, ("group", "path")))
    return jax.shard_map(
        per_device, mesh=mesh, in_specs=in_specs, out_specs=out_specs, check_vma=False
    )
```
